32 devices in a mesh: parts: 2 (over y), seq: 4 (over z), tp: 4 (over x, core).
Axes of the slice: x: 2, y: 2, z: 4, core: 2. Of those that a mesh axis runs over, the one named last changes fastest.
Arguments:
- x_gate: bfloat16 [1024, 4096], P(('parts', 'seq'), 'tp'), parts along dimension 0, may hold values from -6 to 6
- x_key: bfloat16 [1024, 4096], P(('parts', 'seq'), 'tp'), parts along dimension 0, may hold values from -6 to 6
- x_value: bfloat16 [1024, 4096], P(('parts', 'seq'), 'tp'), parts along dimension 0, may hold values from -6 to 6
- conv_state: bfloat16 [254, 4096], P('parts', 'tp'), parts along dimension 0, may hold values from -6 to 6
- filter_taps: float32 [256, 128], P('tp'), may hold values from -0.875 to 0.875
- decay_rates: float32 [256], P('tp'), may hold values from 0.0005 to 0.1
- skip_gain: float32 [4096], P('tp'), may hold values from -1 to 1
- queries: bfloat16 [1024, 2048], P(('parts', 'seq'), 'tp'), parts along dimension 0, may hold values from -10 to 10
- stretch_keys: bfloat16 [1024, 2048], P(('parts', 'seq'), 'tp'), parts along dimension 0, may hold values from -10 to 10
- stretch_values: bfloat16 [1024, 2048], P(('parts', 'seq'), 'tp'), parts along dimension 0, may hold values from -6 to 6
- cache_keys: bfloat16 [64, 2048], P(('parts', 'seq'), 'tp'), parts along dimension 0, may hold values from -10 to 10
- cache_values: bfloat16 [64, 2048], P(('parts', 'seq'), 'tp'), parts along dimension 0, may hold values from -6 to 6
- prefix_len: int32 [2], P('parts'), parts along dimension 0, may hold values from 16 to 32
Outputs:
- hyena_out: bfloat16 [1024, 4096], P(('parts', 'seq'), 'tp'), parts along dimension 0
- attention_out: bfloat16 [1024, 2048], P(('parts', 'seq'), 'tp'), parts along dimension 0
The draws below stay inside these ranges and needn't reach their ends.
There are 2 independent parts, one for each index of `parts`. The reference program is written for one: setup_inputs(seed, part) draws one part's arguments, and reference() takes and returns one part's arrays. A program takes and returns all parts, laid end to end along the dimension named above; an argument that names none is the same for every part. Nothing has to cross between parts.
Inputs may be any that keep to these rules, and one draw needn't show every extreme that they name: `prefix_len`: the number of leading cached positions that hold keys and values.
All inputs are finite; a program needn't handle non-finite values.
Results may differ from the reference program's by a relative error of at most 0.0056.
Values may be sent and summed in bfloat16 or wider, within the bound.
A program may use at most 128 MiB of HBM per device.

```python
import math
import jax
import jax.numpy as jnp
from jax import lax

CH = 4096
GROUP = 16
GROUPS = 256
TAPS = 128
HEADS = 16
HD = 128
TOKENS = 512
CACHE = 32


def draw_queries(key, part):
    base = jax.random.normal(jax.random.fold_in(key, 11), (TOKENS, HEADS * HD), jnp.float32) * 1.73
    return jnp.clip(base, -10.0, 10.0).astype(jnp.bfloat16)


def draw_stretch_keys(key, part):
    base = jax.random.normal(jax.random.fold_in(key, 31), (TOKENS, HEADS * HD), jnp.float32) * 1.73
    return jnp.clip(base, -10.0, 10.0).astype(jnp.bfloat16)


def draw_cache_keys(key, part):
    base = jax.random.normal(jax.random.fold_in(key, 21), (CACHE, HEADS * HD), jnp.float32) * 1.73
    return jnp.clip(base, -10.0, 10.0).astype(jnp.bfloat16)


def draw_decay_rates(key, part):
    return jnp.exp(jax.random.uniform(jax.random.fold_in(key, 44), (GROUPS,), jnp.float32, math.log(0.002), math.log(0.1)))


def block_scale(rng, dims, split, least, largest):
    loudness, own = 1.0, jax.random.fold_in(rng, 6)
    for axis_at, blocks in split:
        steps = jnp.exp(jax.random.uniform(jax.random.fold_in(own, axis_at), (blocks,), jnp.float32, least / len(split), largest / len(split)))
        loudness = loudness * jnp.repeat(steps, dims[axis_at] // blocks).reshape([-1 if axis == axis_at else 1 for axis in range(len(dims))])
    return loudness


def gaussian(key, dims, scale, most, split=(), kind=jnp.bfloat16):
    factor_of = block_scale(key, dims, split, -0.22, 0.18) if split else 1.0
    values = jax.random.normal(key, dims, jnp.float32) * scale * factor_of
    return jnp.minimum(jnp.maximum(values, -most), most).astype(kind)


def setup_inputs(seed: int = 0, part: int = 0) -> dict:
    streams_of = jax.random.split(jax.random.key(seed), 14)
    part_splits = jax.random.split(jax.random.fold_in(streams_of[13], part), 14)
    x_gate = gaussian(part_splits[0], (TOKENS, CH), 1.0, 6.0, ((0, 4), (1, 4)))
    x_key = gaussian(part_splits[1], (TOKENS, CH), 1.0, 6.0, ((0, 4), (1, 4)))
    x_value = gaussian(part_splits[2], (TOKENS, CH), 1.0, 6.0, ((0, 4), (1, 4)))
    conv_state = gaussian(part_splits[3], (TAPS - 1, CH), 1.0, 6.0, ((1, 4),))
    filter_taps = gaussian(streams_of[4], (GROUPS, TAPS), 48 ** -0.5, 0.875, ((0, 4),), jnp.float32)
    decay_rates = draw_decay_rates(jax.random.fold_in(streams_of[13], 71), part)
    skip_gain = jnp.clip(jax.random.uniform(streams_of[6], (CH,), jnp.float32, -1.0, 1.0) * block_scale(streams_of[6], (CH,), ((0, 4),), -0.4, 0.0), -1.0, 1.0)
    queries = draw_queries(jax.random.fold_in(jax.random.fold_in(streams_of[13], part), 71), part)
    stretch_keys = draw_stretch_keys(jax.random.fold_in(jax.random.fold_in(streams_of[13], part), 71), part)
    stretch_values = gaussian(part_splits[9], (TOKENS, HEADS * HD), 1.0, 6.0, ((0, 4), (1, 4)))
    cache_keys = draw_cache_keys(jax.random.fold_in(jax.random.fold_in(streams_of[13], part), 71), part)
    cache_values = gaussian(part_splits[11], (CACHE, HEADS * HD), 1.0, 6.0, ((0, 4), (1, 4)))
    prefix_len = jax.random.randint(part_splits[12], (1,), CACHE // 2, CACHE + 1).astype(jnp.int32)
    return dict(x_gate=x_gate, x_key=x_key, x_value=x_value, conv_state=conv_state, filter_taps=filter_taps, decay_rates=decay_rates, skip_gain=skip_gain, queries=queries, stretch_keys=stretch_keys, stretch_values=stretch_values, cache_keys=cache_keys, cache_values=cache_values, prefix_len=prefix_len)


def reference(x_gate, x_key, x_value, conv_state, filter_taps, decay_rates, skip_gain, queries, stretch_keys, stretch_values, cache_keys, cache_values, prefix_len):
    product_in = (x_key.astype(jnp.float32) * x_value.astype(jnp.float32)).astype(jnp.bfloat16)
    filter_reach = TAPS - 1
    extended = jnp.concatenate([conv_state, product_in], axis=0).astype(jnp.float32)
    tap_ramp = jnp.arange(TAPS).astype(jnp.float32)
    filters = (filter_taps * jnp.exp(-decay_rates[:, None] * tap_ramp[None, :])).astype(jnp.bfloat16)
    per_channel = jnp.repeat(filters, GROUP, axis=0).astype(jnp.float32)

    def add_tap(tap_index, running):
        start_row = jnp.asarray(filter_reach, jnp.int32) - tap_index.astype(jnp.int32)
        window = lax.dynamic_slice_in_dim(extended, start_row, TOKENS, 0)
        column = lax.dynamic_index_in_dim(per_channel, tap_index.astype(jnp.int32), 1, keepdims=False)
        return running + window * column[None, :]
    filtered = lax.fori_loop(0, TAPS, add_tap, jnp.zeros((TOKENS, CH), jnp.float32))
    hyena_out = (x_gate.astype(jnp.float32) * (filtered + skip_gain[None, :] * product_in.astype(jnp.float32))).astype(jnp.bfloat16)
    scale_factor = 1.0 / math.sqrt(HD)
    key_all = jnp.concatenate([cache_keys, stretch_keys], axis=0)
    value_all = jnp.concatenate([cache_values, stretch_values], axis=0)
    query_heads = queries.reshape(TOKENS, HEADS, HD).transpose(1, 0, 2)
    key_heads = key_all.reshape(CACHE + TOKENS, HEADS, HD).transpose(1, 0, 2)
    value_heads = value_all.reshape(CACHE + TOKENS, HEADS, HD).transpose(1, 0, 2)
    key_index = jnp.arange(CACHE + TOKENS).astype(jnp.int32)
    row_index = jnp.arange(TOKENS).astype(jnp.int32)
    cache_ok = (key_index < prefix_len[0])[None, :]
    stretch_ok = (key_index - CACHE)[None, :] <= row_index[:, None]
    allowed = jnp.where((key_index < CACHE)[None, :], cache_ok, stretch_ok)

    def one_head(operands):
        query_rows, key_rows, value_rows = operands
        scores = jnp.dot(query_rows, key_rows.T, preferred_element_type=jnp.float32) * scale_factor
        scores = jnp.where(allowed, scores, -jnp.inf)
        top_score = lax.optimization_barrier(jnp.max(scores, axis=1, keepdims=True))
        weights = jnp.where(allowed, jnp.exp(scores - top_score), 0.0)
        totals = lax.optimization_barrier(jnp.sum(weights, axis=1, keepdims=True))
        mixed_rows = jnp.dot(weights.astype(jnp.bfloat16), value_rows, preferred_element_type=jnp.float32)
        return (mixed_rows / totals).astype(jnp.bfloat16)
    per_head = lax.map(one_head, (query_heads, key_heads, value_heads))
    attention_out = per_head.transpose(1, 0, 2).reshape(TOKENS, HEADS * HD)
    return (hyena_out, attention_out)
```

```python
import math

import jax
import jax.numpy as jnp
from jax import lax
from jax.experimental import pallas as pl
from jax.experimental.pallas import tpu as pltpu
from jax.sharding import PartitionSpec as P

HD = 128


far_position = 1 << 30


def shifted(value, axis, steps):
    count = lax.axis_size(axis)
    first, last = (max(0, -steps), min(count, count - steps))
    return lax.ppermute(value, axis, [(source, source + steps) for source in range(first, last)])


def general_form(
    x_gate,
    x_key,
    x_value,
    conv_state,
    filter_taps,
    decay_rates,
    skip_gain,
    queries,
    stretch_keys,
    stretch_values,
    cache_keys,
    cache_values,
    prefix_len,
):
    rows_dev = x_gate.shape[0]
    chans_dev = x_gate.shape[1]
    seq_index = lax.axis_index("seq")
    product_in = (x_key.astype(jnp.float32) * x_value.astype(jnp.float32)).astype(jnp.bfloat16)
    filter_reach = filter_taps.shape[1] - 1
    received = []
    taken = min(rows_dev, filter_reach)
    received.insert(0, shifted(product_in[rows_dev - taken :], "seq", 1))
    earlier = received[0]
    padded_state = jnp.concatenate(
        [conv_state, jnp.zeros((filter_reach, chans_dev), jnp.bfloat16)], axis=0
    )
    earlier = earlier + lax.dynamic_slice_in_dim(
        padded_state, seq_index * rows_dev, filter_reach, 0
    )
    extended = jnp.concatenate([earlier, product_in], axis=0)
    span_total = rows_dev + filter_reach
    tap_ramp = lax.iota(jnp.float32, filter_reach + 1)
    filters = (filter_taps * jnp.exp(-decay_rates[:, None] * tap_ramp[None, :])).astype(
        jnp.bfloat16
    )
    group_count = filters.shape[0]
    group_width = chans_dev // group_count
    skew_period = span_total + rows_dev - 1
    reversed_taps = jnp.concatenate(
        [filters[:, ::-1], jnp.zeros((group_count, skew_period - filter_reach - 1), jnp.bfloat16)],
        axis=1,
    )
    group_block = min(group_count, 16)
    conv_parts = []
    for first_group in range(0, group_count, group_block):
        taps_block = reversed_taps[first_group : first_group + group_block]
        toeplitz = jnp.tile(taps_block, (1, rows_dev + 1))[:, : rows_dev * (skew_period - 1)]
        toeplitz = toeplitz.reshape(group_block, rows_dev, skew_period - 1)[:, :, :span_total]
        columns = extended[:, first_group * group_width : (first_group + group_block) * group_width]
        columns = columns.reshape(span_total, group_block, group_width)
        conv_block = jnp.einsum(
            "gts,sgc->tgc", toeplitz, columns, preferred_element_type=jnp.float32
        )
        conv_parts.append(conv_block.reshape(rows_dev, group_block * group_width))
    filtered = jnp.concatenate(conv_parts, axis=1)
    hyena_out = (
        x_gate.astype(jnp.float32)
        * (filtered + skip_gain[None, :] * product_in.astype(jnp.float32))
    ).astype(jnp.bfloat16)
    head_count = queries.shape[1] // HD
    half_rows = rows_dev // 2
    scale_factor = 1.0 / math.sqrt(HD)
    half_ramp = lax.iota(jnp.int32, half_rows)
    second_base = seq_index * rows_dev + half_rows
    query_pos = jnp.stack([seq_index * rows_dev + half_ramp, second_base + half_ramp])
    query_heads = queries.reshape(2, half_rows, head_count, HD)
    limit_len = prefix_len[0]

    def consume(state, key_rows, value_rows, key_pos):
        row_total = key_rows.shape[0]
        if row_total <= 512:
            block_rows = row_total
            block_count = 1
        else:
            block_rows = 512
            block_count = -(-row_total // 512)
        key_blocks = key_rows.reshape(block_count, block_rows, head_count, HD)
        value_blocks = value_rows.reshape(block_count, block_rows, head_count, HD)
        pos_blocks = key_pos.reshape(block_count, block_rows)

        def one_block(block_step, inner):
            maxima, totals, sums = inner
            key_block = lax.dynamic_index_in_dim(key_blocks, block_step, 0, keepdims=False)
            value_block = lax.dynamic_index_in_dim(value_blocks, block_step, 0, keepdims=False)
            pos_block = lax.dynamic_index_in_dim(pos_blocks, block_step, 0, keepdims=False)
            for half_index in range(2):
                half_queries = query_heads[half_index]
                half_pos = query_pos[half_index]

                def update(parts):
                    run_max, run_total, run_sum = parts
                    scores = (
                        jnp.einsum(
                            "thd,shd->hts",
                            half_queries,
                            key_block,
                            preferred_element_type=jnp.float32,
                        )
                        * scale_factor
                    )
                    allowed = (pos_block[None, :] <= half_pos[:, None])[None]
                    scores = jnp.where(allowed, scores, -1e30)
                    new_max = jnp.maximum(run_max, jnp.max(scores, axis=2))
                    weights = jnp.where(allowed, jnp.exp(scores - new_max[:, :, None]), 0.0)
                    factor = jnp.exp(run_max - new_max)
                    new_total = run_total * factor + jnp.sum(weights, axis=2)
                    new_sum = run_sum * factor[:, :, None] + jnp.einsum(
                        "hts,shd->htd",
                        weights.astype(jnp.bfloat16),
                        value_block,
                        preferred_element_type=jnp.float32,
                    )
                    return (new_max, new_total, new_sum)

                def unchanged(parts):
                    return parts

                result = lax.cond(
                    jnp.min(pos_block) <= jnp.max(half_pos),
                    update,
                    unchanged,
                    (maxima[half_index], totals[half_index], sums[half_index]),
                )
                maxima = maxima.at[half_index].set(result[0])
                totals = totals.at[half_index].set(result[1])
                sums = sums.at[half_index].set(result[2])
            return (maxima, totals, sums)

        return lax.fori_loop(0, block_count, one_block, state)

    initial = (
        jnp.full((2, head_count, half_rows), -1e30, jnp.float32),
        jnp.zeros((2, head_count, half_rows), jnp.float32),
        jnp.zeros((2, head_count, half_rows, HD), jnp.float32),
    )
    cache_whole = (
        lax.all_gather(cache_keys, "seq", axis=0, tiled=True),
        lax.all_gather(cache_values, "seq", axis=0, tiled=True),
    )
    cache_ids = lax.iota(jnp.int32, cache_whole[0].shape[0])
    cache_pos = jnp.where(cache_ids < limit_len, -1, far_position)
    start_state = consume(initial, cache_whole[0], cache_whole[1], cache_pos)
    piece = (
        lax.all_gather(stretch_keys, "seq", axis=0, tiled=True),
        lax.all_gather(stretch_values, "seq", axis=0, tiled=True),
    )
    key_pos = lax.iota(jnp.int32, piece[0].shape[0])
    state = consume(start_state, piece[0], piece[1], key_pos)
    normalized = state[2] / state[1][:, :, :, None]
    result_rows = (
        normalized.transpose(0, 2, 1, 3).reshape(rows_dev, head_count * HD).astype(jnp.bfloat16)
    )
    return (hyena_out, result_rows)


MESH = pl.DeviceIdType.MESH
F32 = jnp.float32
BF16 = jnp.bfloat16


def remote(src, dst, send_sem, recv_sem, target):
    return pltpu.make_async_remote_copy(
        src_ref=src,
        dst_ref=dst,
        send_sem=send_sem,
        recv_sem=recv_sem,
        device_id={"seq": target},
        device_id_type=MESH,
    )


def short_kernel(
    x_gate, x_key, x_value, conv_state, filter_taps, decay_rates, skip_gain,
    queries, stretch_keys, stretch_values, cache_keys, cache_values, prefix_len,
    hyena_out, attention_out,
    gate_v, key_v, value_v, state_v, taps_v, decay_v, skip_v, q_v, k_v, v_v,
    cache_k, cache_v, k_in, v_in, q_in, product_v, earlier_v, shifted_v,
    reversed_v, lower_v, upper_v, local_v, out_v,
    own_acc, own_stat, part_out, stat_out, part_in, stat_in, att_v,
    load_sem, send_sem, recv_sem, cache_send, cache_recv, out_sem,
):
    me = lax.axis_index("seq")
    rows, chans = gate_v.shape
    groups, taps = taps_v.shape
    width = chans // groups
    heads = q_v.shape[1] // HD
    scale_factor = 1.0 / math.sqrt(HD)

    loads = {}
    for at, (name, src, dst) in enumerate(
        [
            ("key", x_key, key_v),
            ("value", x_value, value_v),
            ("taps", filter_taps, taps_v),
            ("decay", decay_rates, decay_v),
            ("q", queries, q_v),
            ("k", stretch_keys, k_v),
            ("v", stretch_values, v_v),
            ("skip", skip_gain, skip_v),
            ("gate", x_gate, gate_v),
            ("state", conv_state, state_v),
            ("ck", cache_keys, cache_k.at[me]),
            ("cv", cache_values, cache_v.at[me]),
        ]
    ):
        loads[name] = pltpu.make_async_copy(src, dst, load_sem.at[at])
        loads[name].start()

    barrier = pltpu.get_barrier_semaphore()
    for step in range(1, 4):
        pl.semaphore_signal(
            barrier, inc=1, device_id={"seq": lax.rem(me + step, 4)}, device_id_type=MESH
        )
    pl.semaphore_wait(barrier, 3)

    send_k = remote(stretch_keys, k_in, send_sem.at[0], recv_sem.at[0], 1)
    send_v = remote(stretch_values, v_in, send_sem.at[1], recv_sem.at[1], 1)
    send_q2 = remote(queries, q_in.at[0], send_sem.at[2], recv_sem.at[2], 1)
    send_q3 = remote(queries, q_in.at[1], send_sem.at[3], recv_sem.at[3], 1)
    send_q3_near = remote(queries, q_in.at[1], send_sem.at[2], recv_sem.at[3], 2)
    send_product = remote(
        product_v, earlier_v, send_sem.at[4], recv_sem.at[4], lax.rem(me + 1, 4)
    )
    send_part_near = remote(part_out.at[0], part_in.at[0], send_sem.at[5], recv_sem.at[5], 2)
    send_stat_near = remote(stat_out.at[0], stat_in.at[0], send_sem.at[6], recv_sem.at[6], 2)
    send_part_far = remote(part_out.at[1], part_in.at[0], send_sem.at[7], recv_sem.at[5], 3)
    send_stat_far = remote(stat_out.at[1], stat_in.at[0], send_sem.at[8], recv_sem.at[6], 3)
    send_part_last = remote(part_out.at[1], part_in.at[1], send_sem.at[5], recv_sem.at[7], 3)
    send_stat_last = remote(stat_out.at[1], stat_in.at[1], send_sem.at[6], recv_sem.at[8], 3)

    @pl.when(me == 0)
    def _():
        send_k.start()
        send_v.start()

    @pl.when(me == 2)
    def _():
        send_q2.start()

    @pl.when(me == 3)
    def _():
        send_q3.start()
        send_q3_near.start()

    cache_copies = []
    for step in range(1, 4):
        target = lax.rem(me + step, 4)
        for which, (src, dst) in enumerate(
            [(cache_keys, cache_k), (cache_values, cache_v)]
        ):
            copy = remote(
                src, dst.at[me], cache_send.at[which, step - 1], cache_recv.at[which, me], target
            )
            copy.start()
            cache_copies.append(copy)

    loads["key"].wait()
    loads["value"].wait()
    product_v[...] = (key_v[...].astype(F32) * value_v[...].astype(F32)).astype(BF16)

    @pl.when(me < 3)
    def _():
        send_product.start()

    loads["taps"].wait()
    loads["decay"].wait()
    row_id = lax.broadcasted_iota(jnp.int32, (groups, groups), 0)
    col_id = lax.broadcasted_iota(jnp.int32, (groups, groups), 1)
    rates = jnp.sum(
        jnp.where(row_id == col_id, decay_v[...], 0.0), axis=1, keepdims=True
    )
    ramp = lax.broadcasted_iota(jnp.int32, (groups, taps), 1).astype(F32)
    filters = (taps_v[...] * jnp.exp(-rates * ramp)).astype(BF16)
    from_id = lax.broadcasted_iota(jnp.int32, (taps, taps), 0)
    to_id = lax.broadcasted_iota(jnp.int32, (taps, taps), 1)
    total_id = from_id + to_id
    flip = jnp.where((total_id == 0) | (total_id == taps), 1.0, 0.0).astype(BF16)
    reversed_v[...] = jnp.dot(filters, flip, preferred_element_type=F32)
    below = to_id <= from_id

    def build(pair, carry):
        for half in range(2):
            row = reversed_v[pl.ds(pair * 2 + half, 1), :]
            circ = pltpu.roll(
                jnp.broadcast_to(row, (rows, taps)), 0, 1, stride=1, stride_axis=0
            )
            lanes = pl.ds(half * taps, taps)
            lower_v[pair, :, lanes] = jnp.where(below, circ, 0.0).astype(BF16)
            upper_v[pair, :, lanes] = jnp.where(below, 0.0, circ).astype(BF16)
        return carry

    lax.fori_loop(0, groups // 2, build, 0)

    lane = lax.broadcasted_iota(jnp.int32, (1, 128), 1)
    odd_lane = lax.rem(lane // width, 2) == 1
    odd = jnp.where(odd_lane, 1.0, 0.0).astype(BF16)
    even = jnp.where(odd_lane, 0.0, 1.0).astype(BF16)
    pair_of = lax.broadcasted_iota(jnp.int32, (rows, 128), 1) // (2 * width)
    pairs = 128 // (2 * width)

    def filtered(matrix_ref, block, tile):
        stacked = jnp.concatenate([block * even, block * odd], axis=0)
        total = None
        for at in range(pairs):
            term = jnp.dot(
                matrix_ref[tile * pairs + at], stacked, preferred_element_type=F32
            )
            total = term if total is None else jnp.where(pair_of == at, term, total)
        return total

    loads["skip"].wait()
    for tile in range(chans // 128):
        cols = slice(tile * 128, (tile + 1) * 128)
        block = product_v[:, cols]
        local_v[:, cols] = filtered(lower_v, block, tile) + skip_v[:, cols] * block.astype(F32)

    loads["q"].wait()
    loads["k"].wait()
    loads["v"].wait()
    loads["ck"].wait()
    loads["cv"].wait()
    for step in range(1, 4):
        source = lax.rem(me + step, 4)
        for which, (src, dst) in enumerate(
            [(cache_keys, cache_k), (cache_values, cache_v)]
        ):
            remote(
                src, dst.at[source], cache_send.at[which, step - 1],
                cache_recv.at[which, source], source,
            ).wait_recv()

    def joined(ref, cols):
        return jnp.concatenate(
            [ref[at, :, cols].astype(F32) for at in range(4)], axis=0
        ).astype(BF16)

    cache_rows = 4 * cache_k.shape[1]
    causal = to_id >= from_id
    in_prefix = (
        lax.broadcasted_iota(jnp.int32, (cache_rows, rows), 0) < prefix_len[0]
    )

    def attend(query, blocks):
        scores = []
        for key, value, allowed in blocks:
            score = (
                lax.dot_general(
                    key, query, (((1,), (1,)), ((), ())), preferred_element_type=F32
                )
                * scale_factor
            )
            if allowed is not None:
                score = jnp.where(allowed, score, -1e30)
            scores.append(score)
        top = jnp.max(scores[0], axis=0, keepdims=True)
        for score in scores[1:]:
            top = jnp.maximum(top, jnp.max(score, axis=0, keepdims=True))
        total, mixed = 0.0, 0.0
        for score, (key, value, allowed) in zip(scores, blocks):
            weight = jnp.exp(score - top)
            if allowed is not None:
                weight = jnp.where(allowed, weight, 0.0)
            total = total + jnp.sum(weight, axis=0, keepdims=True)
            mixed = mixed + lax.dot_general(
                value, weight.astype(BF16), (((0,), (0,)), ((), ())),
                preferred_element_type=F32,
            )
        return top, total, mixed

    def head_cols(head):
        return slice(head * HD, (head + 1) * HD)

    def own_blocks(head):
        cols = head_cols(head)
        return [
            (joined(cache_k, cols), joined(cache_v, cols), in_prefix),
            (k_v[:, cols], v_v[:, cols], causal),
        ]

    def keep(head, result):
        own_stat[head : head + 1, :] = result[0]
        own_stat[heads + head : heads + head + 1, :] = result[1]
        own_acc[head] = result[2]

    def give(slot, head, result):
        stat_out[slot, head : head + 1, :] = result[0]
        stat_out[slot, heads + head : heads + head + 1, :] = result[1]
        part_out[slot, head] = (result[2] / result[1]).astype(BF16)

    @pl.when(me != 1)
    def _():
        for head in range(heads):
            keep(head, attend(q_v[:, head_cols(head)], own_blocks(head)))

    @pl.when(me == 1)
    def _():
        send_k.wait_recv()
        send_v.wait_recv()

        def shared_blocks(cols):
            return [
                (k_in[:, cols], v_in[:, cols], None),
                (k_v[:, cols], v_v[:, cols], None),
            ]

        for slot, arrival, part, stat in (
            (1, send_q3, send_part_far, send_stat_far),
            (0, send_q2, send_part_near, send_stat_near),
        ):
            arrival.wait_recv()
            for head in range(heads):
                cols = head_cols(head)
                give(slot, head, attend(q_in[slot, :, cols], shared_blocks(cols)))
            part.start()
            stat.start()
        for head in range(heads):
            cols = head_cols(head)
            keep(
                head,
                attend(
                    q_v[:, cols], own_blocks(head) + [(k_in[:, cols], v_in[:, cols], None)]
                ),
            )

    @pl.when(me == 2)
    def _():
        send_q3_near.wait_recv()
        for head in range(heads):
            cols = head_cols(head)
            give(1, head, attend(q_in[1, :, cols], [(k_v[:, cols], v_v[:, cols], None)]))
        send_part_last.start()
        send_stat_last.start()

    loads["state"].wait()

    @pl.when(me == 0)
    def _():
        shifted_v[0:1, :] = jnp.zeros((1, chans), F32)
        shifted_v[pl.ds(1, rows - 1), :] = state_v[...].astype(F32)
        earlier_v[...] = shifted_v[...].astype(BF16)

    @pl.when(me > 0)
    def _():
        send_product.wait_recv()

    loads["gate"].wait()
    for tile in range(chans // 128):
        cols = slice(tile * 128, (tile + 1) * 128)
        whole = local_v[:, cols] + filtered(upper_v, earlier_v[:, cols], tile)
        out_v[:, cols] = (gate_v[:, cols].astype(F32) * whole).astype(BF16)
    hyena_write = pltpu.make_async_copy(out_v, hyena_out, out_sem.at[0])
    hyena_write.start()

    def finish(slots):
        for head in range(heads):
            top = own_stat[head : head + 1, :]
            tops = [stat_in[slot, head : head + 1, :] for slot in slots]
            best = top
            for other in tops:
                best = jnp.maximum(best, other)
            share = jnp.exp(top - best)
            total = own_stat[heads + head : heads + head + 1, :] * share
            mixed = own_acc[head] * share
            for slot, other in zip(slots, tops):
                share = stat_in[slot, heads + head : heads + head + 1, :] * jnp.exp(other - best)
                total = total + share
                mixed = mixed + part_in[slot, head].astype(F32) * share
            att_v[:, head_cols(head)] = (mixed / total).T.astype(BF16)

    @pl.when(me < 2)
    def _():
        finish([])

    @pl.when(me == 2)
    def _():
        send_part_near.wait_recv()
        send_stat_near.wait_recv()
        finish([0])

    @pl.when(me == 3)
    def _():
        send_part_last.wait_recv()
        send_stat_last.wait_recv()
        send_part_far.wait_recv()
        send_stat_far.wait_recv()
        finish([0, 1])

    attention_write = pltpu.make_async_copy(att_v, attention_out, out_sem.at[1])
    attention_write.start()

    for copy in cache_copies:
        copy.wait_send()

    @pl.when(me < 3)
    def _():
        send_product.wait_send()

    @pl.when(me == 0)
    def _():
        send_k.wait_send()
        send_v.wait_send()

    @pl.when(me == 1)
    def _():
        for copy in (send_part_near, send_stat_near, send_part_far, send_stat_far):
            copy.wait_send()

    @pl.when(me == 2)
    def _():
        for copy in (send_q2, send_part_last, send_stat_last):
            copy.wait_send()

    @pl.when(me == 3)
    def _():
        send_q3.wait_send()
        send_q3_near.wait_send()

    hyena_write.wait()
    attention_write.wait()


def short_form(
    x_gate, x_key, x_value, conv_state, filter_taps, decay_rates, skip_gain,
    queries, stretch_keys, stretch_values, cache_keys, cache_values, prefix_len,
):
    rows, chans = x_gate.shape
    groups, taps = filter_taps.shape
    across = queries.shape[1]
    heads = across // HD
    cache_rows = cache_keys.shape[0]
    any_spec = pl.BlockSpec(memory_space=pltpu.HBM)
    dma = pltpu.SemaphoreType.DMA
    vm = pltpu.VMEM
    return pl.pallas_call(
        short_kernel,
        out_shape=(
            jax.ShapeDtypeStruct((rows, chans), BF16),
            jax.ShapeDtypeStruct((rows, across), BF16),
        ),
        in_specs=[any_spec] * 12 + [pl.BlockSpec(memory_space=pltpu.SMEM)],
        out_specs=(any_spec, any_spec),
        scratch_shapes=[
            vm((rows, chans), BF16),
            vm((rows, chans), BF16),
            vm((rows, chans), BF16),
            vm((rows - 1, chans), BF16),
            vm((groups, taps), F32),
            vm((1, groups), F32),
            vm((1, chans), F32),
            vm((rows, across), BF16),
            vm((rows, across), BF16),
            vm((rows, across), BF16),
            vm((4, cache_rows, across), BF16),
            vm((4, cache_rows, across), BF16),
            vm((rows, across), BF16),
            vm((rows, across), BF16),
            vm((2, rows, across), BF16),
            vm((rows, chans), BF16),
            vm((rows, chans), BF16),
            vm((rows, chans), F32),
            vm((groups, taps), F32),
            vm((groups // 2, rows, 2 * taps), BF16),
            vm((groups // 2, rows, 2 * taps), BF16),
            vm((rows, chans), F32),
            vm((rows, chans), BF16),
            vm((heads, HD, rows), F32),
            vm((2 * heads, rows), F32),
            vm((2, heads, HD, rows), BF16),
            vm((2, 2 * heads, rows), F32),
            vm((2, heads, HD, rows), BF16),
            vm((2, 2 * heads, rows), F32),
            vm((rows, across), BF16),
            dma((12,)),
            dma((9,)),
            dma((9,)),
            dma((2, 3)),
            dma((2, 4)),
            dma((2,)),
        ],
        compiler_params=pltpu.CompilerParams(
            collective_id=0, has_side_effects=True, vmem_limit_bytes=48 << 20
        ),
    )(
        x_gate, x_key, x_value, conv_state, filter_taps,
        decay_rates.reshape(1, groups), skip_gain.reshape(1, chans),
        queries, stretch_keys, stretch_values, cache_keys, cache_values, prefix_len,
    )


def on_device(*arrays):
    rows, taps = arrays[0].shape[0], arrays[4].shape[1]
    if lax.axis_size("seq") == 4 and rows == taps == 128:
        return short_form(*arrays)
    return general_form(*arrays)


def solution(mesh):
    placed = (
        P(("parts", "seq"), "tp"),
        P(("parts", "seq"), "tp"),
        P(("parts", "seq"), "tp"),
        P("parts", "tp"),
        P("tp", None),
        P("tp"),
        P("tp"),
        P(("parts", "seq"), "tp"),
        P(("parts", "seq"), "tp"),
        P(("parts", "seq"), "tp"),
        P(("parts", "seq"), "tp"),
        P(("parts", "seq"), "tp"),
        P("parts"),
    )
    return jax.shard_map(
        on_device,
        mesh=mesh,
        in_specs=placed,
        out_specs=(P(("parts", "seq"), "tp"), P(("parts", "seq"), "tp")),
        check_vma=False,
    )
```

```python
import math

import jax
import jax.numpy as jnp
from jax import lax
from jax.experimental import pallas as pl
from jax.experimental.pallas import tpu as pltpu
from jax.sharding import PartitionSpec as P

HD = 128


far_position = 1 << 30


def shifted(value, axis, steps):
    count = lax.axis_size(axis)
    first, last = (max(0, -steps), min(count, count - steps))
    return lax.ppermute(value, axis, [(source, source + steps) for source in range(first, last)])


def general_form(
    x_gate,
    x_key,
    x_value,
    conv_state,
    filter_taps,
    decay_rates,
    skip_gain,
    queries,
    stretch_keys,
    stretch_values,
    cache_keys,
    cache_values,
    prefix_len,
):
    rows_dev = x_gate.shape[0]
    chans_dev = x_gate.shape[1]
    seq_index = lax.axis_index("seq")
    product_in = (x_key.astype(jnp.float32) * x_value.astype(jnp.float32)).astype(jnp.bfloat16)
    filter_reach = filter_taps.shape[1] - 1
    received = []
    taken = min(rows_dev, filter_reach)
    received.insert(0, shifted(product_in[rows_dev - taken :], "seq", 1))
    earlier = received[0]
    padded_state = jnp.concatenate(
        [conv_state, jnp.zeros((filter_reach, chans_dev), jnp.bfloat16)], axis=0
    )
    earlier = earlier + lax.dynamic_slice_in_dim(
        padded_state, seq_index * rows_dev, filter_reach, 0
    )
    extended = jnp.concatenate([earlier, product_in], axis=0)
    span_total = rows_dev + filter_reach
    tap_ramp = lax.iota(jnp.float32, filter_reach + 1)
    filters = (filter_taps * jnp.exp(-decay_rates[:, None] * tap_ramp[None, :])).astype(
        jnp.bfloat16
    )
    group_count = filters.shape[0]
    group_width = chans_dev // group_count
    skew_period = span_total + rows_dev - 1
    reversed_taps = jnp.concatenate(
        [filters[:, ::-1], jnp.zeros((group_count, skew_period - filter_reach - 1), jnp.bfloat16)],
        axis=1,
    )
    group_block = min(group_count, 16)
    conv_parts = []
    for first_group in range(0, group_count, group_block):
        taps_block = reversed_taps[first_group : first_group + group_block]
        toeplitz = jnp.tile(taps_block, (1, rows_dev + 1))[:, : rows_dev * (skew_period - 1)]
        toeplitz = toeplitz.reshape(group_block, rows_dev, skew_period - 1)[:, :, :span_total]
        columns = extended[:, first_group * group_width : (first_group + group_block) * group_width]
        columns = columns.reshape(span_total, group_block, group_width)
        conv_block = jnp.einsum(
            "gts,sgc->tgc", toeplitz, columns, preferred_element_type=jnp.float32
        )
        conv_parts.append(conv_block.reshape(rows_dev, group_block * group_width))
    filtered = jnp.concatenate(conv_parts, axis=1)
    hyena_out = (
        x_gate.astype(jnp.float32)
        * (filtered + skip_gain[None, :] * product_in.astype(jnp.float32))
    ).astype(jnp.bfloat16)
    head_count = queries.shape[1] // HD
    half_rows = rows_dev // 2
    scale_factor = 1.0 / math.sqrt(HD)
    half_ramp = lax.iota(jnp.int32, half_rows)
    second_base = seq_index * rows_dev + half_rows
    query_pos = jnp.stack([seq_index * rows_dev + half_ramp, second_base + half_ramp])
    query_heads = queries.reshape(2, half_rows, head_count, HD)
    limit_len = prefix_len[0]

    def consume(state, key_rows, value_rows, key_pos):
        row_total = key_rows.shape[0]
        if row_total <= 512:
            block_rows = row_total
            block_count = 1
        else:
            block_rows = 512
            block_count = -(-row_total // 512)
        key_blocks = key_rows.reshape(block_count, block_rows, head_count, HD)
        value_blocks = value_rows.reshape(block_count, block_rows, head_count, HD)
        pos_blocks = key_pos.reshape(block_count, block_rows)

        def one_block(block_step, inner):
            maxima, totals, sums = inner
            key_block = lax.dynamic_index_in_dim(key_blocks, block_step, 0, keepdims=False)
            value_block = lax.dynamic_index_in_dim(value_blocks, block_step, 0, keepdims=False)
            pos_block = lax.dynamic_index_in_dim(pos_blocks, block_step, 0, keepdims=False)
            for half_index in range(2):
                half_queries = query_heads[half_index]
                half_pos = query_pos[half_index]

                def update(parts):
                    run_max, run_total, run_sum = parts
                    scores = (
                        jnp.einsum(
                            "thd,shd->hts",
                            half_queries,
                            key_block,
                            preferred_element_type=jnp.float32,
                        )
                        * scale_factor
                    )
                    allowed = (pos_block[None, :] <= half_pos[:, None])[None]
                    scores = jnp.where(allowed, scores, -1e30)
                    new_max = jnp.maximum(run_max, jnp.max(scores, axis=2))
                    weights = jnp.where(allowed, jnp.exp(scores - new_max[:, :, None]), 0.0)
                    factor = jnp.exp(run_max - new_max)
                    new_total = run_total * factor + jnp.sum(weights, axis=2)
                    new_sum = run_sum * factor[:, :, None] + jnp.einsum(
                        "hts,shd->htd",
                        weights.astype(jnp.bfloat16),
                        value_block,
                        preferred_element_type=jnp.float32,
                    )
                    return (new_max, new_total, new_sum)

                def unchanged(parts):
                    return parts

                result = lax.cond(
                    jnp.min(pos_block) <= jnp.max(half_pos),
                    update,
                    unchanged,
                    (maxima[half_index], totals[half_index], sums[half_index]),
                )
                maxima = maxima.at[half_index].set(result[0])
                totals = totals.at[half_index].set(result[1])
                sums = sums.at[half_index].set(result[2])
            return (maxima, totals, sums)

        return lax.fori_loop(0, block_count, one_block, state)

    initial = (
        jnp.full((2, head_count, half_rows), -1e30, jnp.float32),
        jnp.zeros((2, head_count, half_rows), jnp.float32),
        jnp.zeros((2, head_count, half_rows, HD), jnp.float32),
    )
    cache_whole = (
        lax.all_gather(cache_keys, "seq", axis=0, tiled=True),
        lax.all_gather(cache_values, "seq", axis=0, tiled=True),
    )
    cache_ids = lax.iota(jnp.int32, cache_whole[0].shape[0])
    cache_pos = jnp.where(cache_ids < limit_len, -1, far_position)
    start_state = consume(initial, cache_whole[0], cache_whole[1], cache_pos)
    piece = (
        lax.all_gather(stretch_keys, "seq", axis=0, tiled=True),
        lax.all_gather(stretch_values, "seq", axis=0, tiled=True),
    )
    key_pos = lax.iota(jnp.int32, piece[0].shape[0])
    state = consume(start_state, piece[0], piece[1], key_pos)
    normalized = state[2] / state[1][:, :, :, None]
    result_rows = (
        normalized.transpose(0, 2, 1, 3).reshape(rows_dev, head_count * HD).astype(jnp.bfloat16)
    )
    return (hyena_out, result_rows)


MESH = pl.DeviceIdType.MESH
F32 = jnp.float32
BF16 = jnp.bfloat16


def remote(src, dst, send_sem, recv_sem, target):
    return pltpu.make_async_remote_copy(
        src_ref=src,
        dst_ref=dst,
        send_sem=send_sem,
        recv_sem=recv_sem,
        device_id={"seq": target},
        device_id_type=MESH,
    )


def short_kernel(
    x_gate, x_key, x_value, conv_state, filter_taps, decay_rates, skip_gain,
    queries, stretch_keys, stretch_values, cache_keys, cache_values, prefix_len,
    hyena_out, attention_out,
    gate_v, key_v, value_v, state_v, taps_v, decay_v, skip_v, q_v, k_v, v_v,
    cache_k, cache_v, k_in, v_in, q_in, product_v, earlier_v, shifted_v,
    reversed_v, lower_v, upper_v, local_v, out_v,
    own_acc, own_stat, part_out, stat_out, part_in, stat_in, att_v,
    load_sem, send_sem, recv_sem, cache_send, cache_recv, out_sem,
):
    me = lax.axis_index("seq")
    rows, chans = gate_v.shape
    groups, taps = taps_v.shape
    width = chans // groups
    heads = q_v.shape[1] // HD
    scale_factor = 1.0 / math.sqrt(HD)

    loads = {}
    for at, (name, src, dst) in enumerate(
        [
            ("key", x_key, key_v),
            ("value", x_value, value_v),
            ("taps", filter_taps, taps_v),
            ("decay", decay_rates, decay_v),
            ("q", queries, q_v),
            ("k", stretch_keys, k_v),
            ("v", stretch_values, v_v),
            ("skip", skip_gain, skip_v),
            ("gate", x_gate, gate_v),
            ("state", conv_state, state_v),
            ("ck", cache_keys, cache_k.at[me]),
            ("cv", cache_values, cache_v.at[me]),
        ]
    ):
        loads[name] = pltpu.make_async_copy(src, dst, load_sem.at[at])
        loads[name].start()

    barrier = pltpu.get_barrier_semaphore()
    for step in range(1, 4):
        pl.semaphore_signal(
            barrier, inc=1, device_id={"seq": lax.rem(me + step, 4)}, device_id_type=MESH
        )
    pl.semaphore_wait(barrier, 3)

    send_k = remote(stretch_keys, k_in, send_sem.at[0], recv_sem.at[0], 1)
    send_v = remote(stretch_values, v_in, send_sem.at[1], recv_sem.at[1], 1)
    send_q2 = remote(queries, q_in.at[0], send_sem.at[2], recv_sem.at[2], 1)
    send_q3 = remote(queries, q_in.at[1], send_sem.at[3], recv_sem.at[3], 1)
    send_q3_near = remote(queries, q_in.at[1], send_sem.at[2], recv_sem.at[3], 2)
    send_product = remote(
        product_v, earlier_v, send_sem.at[4], recv_sem.at[4], lax.rem(me + 1, 4)
    )
    send_part_near = remote(part_out.at[0], part_in.at[0], send_sem.at[5], recv_sem.at[5], 2)
    send_stat_near = remote(stat_out.at[0], stat_in.at[0], send_sem.at[6], recv_sem.at[6], 2)
    send_part_far = remote(part_out.at[1], part_in.at[0], send_sem.at[7], recv_sem.at[5], 3)
    send_stat_far = remote(stat_out.at[1], stat_in.at[0], send_sem.at[8], recv_sem.at[6], 3)
    send_part_last = remote(part_out.at[1], part_in.at[1], send_sem.at[5], recv_sem.at[7], 3)
    send_stat_last = remote(stat_out.at[1], stat_in.at[1], send_sem.at[6], recv_sem.at[8], 3)

    @pl.when(me == 0)
    def _():
        send_k.start()
        send_v.start()

    @pl.when(me == 2)
    def _():
        send_q2.start()

    @pl.when(me == 3)
    def _():
        send_q3.start()
        send_q3_near.start()

    cache_copies = []
    for step in range(1, 4):
        target = lax.rem(me + step, 4)
        for which, (src, dst) in enumerate(
            [(cache_keys, cache_k), (cache_values, cache_v)]
        ):
            copy = remote(
                src, dst.at[me], cache_send.at[which, step - 1], cache_recv.at[which, me], target
            )
            copy.start()
            cache_copies.append(copy)

    loads["key"].wait()
    loads["value"].wait()
    product_v[...] = (key_v[...].astype(F32) * value_v[...].astype(F32)).astype(BF16)

    @pl.when(me < 3)
    def _():
        send_product.start()

    loads["taps"].wait()
    loads["decay"].wait()
    row_id = lax.broadcasted_iota(jnp.int32, (groups, groups), 0)
    col_id = lax.broadcasted_iota(jnp.int32, (groups, groups), 1)
    rates = jnp.sum(
        jnp.where(row_id == col_id, decay_v[...], 0.0), axis=1, keepdims=True
    )
    ramp = lax.broadcasted_iota(jnp.int32, (groups, taps), 1).astype(F32)
    filters = (taps_v[...] * jnp.exp(-rates * ramp)).astype(BF16)
    from_id = lax.broadcasted_iota(jnp.int32, (taps, taps), 0)
    to_id = lax.broadcasted_iota(jnp.int32, (taps, taps), 1)
    total_id = from_id + to_id
    flip = jnp.where((total_id == 0) | (total_id == taps), 1.0, 0.0).astype(BF16)
    reversed_v[...] = jnp.dot(filters, flip, preferred_element_type=F32)
    below = to_id <= from_id

    def build(pair, carry):
        for half in range(2):
            row = reversed_v[pl.ds(pair * 2 + half, 1), :]
            circ = pltpu.roll(
                jnp.broadcast_to(row, (rows, taps)), 0, 1, stride=1, stride_axis=0
            )
            lanes = pl.ds(half * taps, taps)
            lower_v[pair, :, lanes] = jnp.where(below, circ, 0.0).astype(BF16)
            upper_v[pair, :, lanes] = jnp.where(below, 0.0, circ).astype(BF16)
        return carry

    lax.fori_loop(0, groups // 2, build, 0)

    lane = lax.broadcasted_iota(jnp.int32, (1, 128), 1)
    odd_lane = lax.rem(lane // width, 2) == 1
    odd = jnp.where(odd_lane, 1.0, 0.0).astype(BF16)
    even = jnp.where(odd_lane, 0.0, 1.0).astype(BF16)
    pair_of = lax.broadcasted_iota(jnp.int32, (rows, 128), 1) // (2 * width)
    pairs = 128 // (2 * width)

    def filtered(matrix_ref, block, tile):
        stacked = jnp.concatenate([block * even, block * odd], axis=0)
        total = None
        for at in range(pairs):
            term = jnp.dot(
                matrix_ref[tile * pairs + at], stacked, preferred_element_type=F32
            )
            total = term if total is None else jnp.where(pair_of == at, term, total)
        return total

    loads["skip"].wait()
    for tile in range(chans // 128):
        cols = slice(tile * 128, (tile + 1) * 128)
        block = product_v[:, cols]
        local_v[:, cols] = filtered(lower_v, block, tile) + skip_v[:, cols] * block.astype(F32)

    loads["q"].wait()
    loads["k"].wait()
    loads["v"].wait()
    loads["ck"].wait()
    loads["cv"].wait()
    for step in range(1, 4):
        source = lax.rem(me + step, 4)
        for which, (src, dst) in enumerate(
            [(cache_keys, cache_k), (cache_values, cache_v)]
        ):
            remote(
                src, dst.at[source], cache_send.at[which, step - 1],
                cache_recv.at[which, source], source,
            ).wait_recv()

    def joined(ref, cols):
        return jnp.concatenate(
            [ref[at, :, cols].astype(F32) for at in range(4)], axis=0
        ).astype(BF16)

    cache_rows = 4 * cache_k.shape[1]
    causal = to_id >= from_id
    in_prefix = (
        lax.broadcasted_iota(jnp.int32, (cache_rows, rows), 0) < prefix_len[0]
    )

    def attend(query, blocks):
        scores = []
        for key, value, allowed in blocks:
            score = (
                lax.dot_general(
                    key, query, (((1,), (1,)), ((), ())), preferred_element_type=F32
                )
                * scale_factor
            )
            if allowed is not None:
                score = jnp.where(allowed, score, -1e30)
            scores.append(score)
        top = jnp.max(scores[0], axis=0, keepdims=True)
        for score in scores[1:]:
            top = jnp.maximum(top, jnp.max(score, axis=0, keepdims=True))
        total, mixed = 0.0, 0.0
        for score, (key, value, allowed) in zip(scores, blocks):
            weight = jnp.exp(score - top)
            if allowed is not None:
                weight = jnp.where(allowed, weight, 0.0)
            total = total + jnp.sum(weight, axis=0, keepdims=True)
            mixed = mixed + lax.dot_general(
                value, weight.astype(BF16), (((0,), (0,)), ((), ())),
                preferred_element_type=F32,
            )
        return top, total, mixed

    def head_cols(head):
        return slice(head * HD, (head + 1) * HD)

    def own_blocks(head):
        cols = head_cols(head)
        return [
            (joined(cache_k, cols), joined(cache_v, cols), in_prefix),
            (k_v[:, cols], v_v[:, cols], causal),
        ]

    def keep(head, result):
        own_stat[head : head + 1, :] = result[0]
        own_stat[heads + head : heads + head + 1, :] = result[1]
        own_acc[head] = result[2]

    def give(slot, head, result):
        stat_out[slot, head : head + 1, :] = result[0]
        stat_out[slot, heads + head : heads + head + 1, :] = result[1]
        part_out[slot, head] = (result[2] / result[1]).astype(BF16)

    @pl.when(me != 1)
    def _():
        for head in range(heads):
            keep(head, attend(q_v[:, head_cols(head)], own_blocks(head)))

    @pl.when(me == 1)
    def _():
        send_k.wait_recv()
        send_v.wait_recv()

        def shared_blocks(cols):
            return [
                (k_in[:, cols], v_in[:, cols], None),
                (k_v[:, cols], v_v[:, cols], None),
            ]

        for slot, arrival, part, stat in (
            (1, send_q3, send_part_far, send_stat_far),
            (0, send_q2, send_part_near, send_stat_near),
        ):
            arrival.wait_recv()
            for head in range(heads):
                cols = head_cols(head)
                give(slot, head, attend(q_in[slot, :, cols], shared_blocks(cols)))
            part.start()
            stat.start()
        for head in range(heads):
            cols = head_cols(head)
            keep(
                head,
                attend(
                    q_v[:, cols], own_blocks(head) + [(k_in[:, cols], v_in[:, cols], None)]
                ),
            )

    @pl.when(me == 2)
    def _():
        send_q3_near.wait_recv()
        for head in range(heads):
            cols = head_cols(head)
            give(1, head, attend(q_in[1, :, cols], [(k_v[:, cols], v_v[:, cols], None)]))
        send_part_last.start()
        send_stat_last.start()

    loads["state"].wait()

    @pl.when(me == 0)
    def _():
        shifted_v[0:1, :] = jnp.zeros((1, chans), F32)
        shifted_v[pl.ds(1, rows - 1), :] = state_v[...].astype(F32)
        earlier_v[...] = shifted_v[...].astype(BF16)

    @pl.when(me > 0)
    def _():
        send_product.wait_recv()

    loads["gate"].wait()
    for tile in range(chans // 128):
        cols = slice(tile * 128, (tile + 1) * 128)
        whole = local_v[:, cols] + filtered(upper_v, earlier_v[:, cols], tile)
        out_v[:, cols] = (gate_v[:, cols].astype(F32) * whole).astype(BF16)
    hyena_write = pltpu.make_async_copy(out_v, hyena_out, out_sem.at[0])
    hyena_write.start()

    def finish(slots):
        for head in range(heads):
            top = own_stat[head : head + 1, :]
            tops = [stat_in[slot, head : head + 1, :] for slot in slots]
            best = top
            for other in tops:
                best = jnp.maximum(best, other)
            share = jnp.exp(top - best)
            total = own_stat[heads + head : heads + head + 1, :] * share
            mixed = own_acc[head] * share
            for slot, other in zip(slots, tops):
                share = stat_in[slot, heads + head : heads + head + 1, :] * jnp.exp(other - best)
                total = total + share
                mixed = mixed + part_in[slot, head].astype(F32) * share
            att_v[:, head_cols(head)] = (mixed / total).T.astype(BF16)

    @pl.when(me < 2)
    def _():
        finish([])

    @pl.when(me == 2)
    def _():
        send_part_near.wait_recv()
        send_stat_near.wait_recv()
        finish([0])

    @pl.when(me == 3)
    def _():
        send_part_last.wait_recv()
        send_stat_last.wait_recv()
        send_part_far.wait_recv()
        send_stat_far.wait_recv()
        finish([0, 1])

    attention_write = pltpu.make_async_copy(att_v, attention_out, out_sem.at[1])
    attention_write.start()

    for copy in cache_copies:
        copy.wait_send()

    @pl.when(me < 3)
    def _():
        send_product.wait_send()

    @pl.when(me == 0)
    def _():
        send_k.wait_send()
        send_v.wait_send()

    @pl.when(me == 1)
    def _():
        for copy in (send_part_near, send_stat_near, send_part_far, send_stat_far):
            copy.wait_send()

    @pl.when(me == 2)
    def _():
        for copy in (send_q2, send_part_last, send_stat_last):
            copy.wait_send()

    @pl.when(me == 3)
    def _():
        send_q3.wait_send()
        send_q3_near.wait_send()

    hyena_write.wait()
    attention_write.wait()


def short_form(
    x_gate, x_key, x_value, conv_state, filter_taps, decay_rates, skip_gain,
    queries, stretch_keys, stretch_values, cache_keys, cache_values, prefix_len,
):
    rows, chans = x_gate.shape
    groups, taps = filter_taps.shape
    across = queries.shape[1]
    heads = across // HD
    cache_rows = cache_keys.shape[0]
    any_spec = pl.BlockSpec(memory_space=pltpu.HBM)
    dma = pltpu.SemaphoreType.DMA
    vm = pltpu.VMEM
    return pl.pallas_call(
        short_kernel,
        out_shape=(
            jax.ShapeDtypeStruct((rows, chans), BF16),
            jax.ShapeDtypeStruct((rows, across), BF16),
        ),
        in_specs=[any_spec] * 12 + [pl.BlockSpec(memory_space=pltpu.SMEM)],
        out_specs=(any_spec, any_spec),
        scratch_shapes=[
            vm((rows, chans), BF16),
            vm((rows, chans), BF16),
            vm((rows, chans), BF16),
            vm((rows - 1, chans), BF16),
            vm((groups, taps), F32),
            vm((1, groups), F32),
            vm((1, chans), F32),
            vm((rows, across), BF16),
            vm((rows, across), BF16),
            vm((rows, across), BF16),
            vm((4, cache_rows, across), BF16),
            vm((4, cache_rows, across), BF16),
            vm((rows, across), BF16),
            vm((rows, across), BF16),
            vm((2, rows, across), BF16),
            vm((rows, chans), BF16),
            vm((rows, chans), BF16),
            vm((rows, chans), F32),
            vm((groups, taps), F32),
            vm((groups // 2, rows, 2 * taps), BF16),
            vm((groups // 2, rows, 2 * taps), BF16),
            vm((rows, chans), F32),
            vm((rows, chans), BF16),
            vm((heads, HD, rows), F32),
            vm((2 * heads, rows), F32),
            vm((2, heads, HD, rows), BF16),
            vm((2, 2 * heads, rows), F32),
            vm((2, heads, HD, rows), BF16),
            vm((2, 2 * heads, rows), F32),
            vm((rows, across), BF16),
            dma((12,)),
            dma((9,)),
            dma((9,)),
            dma((2, 3)),
            dma((2, 4)),
            dma((2,)),
        ],
        compiler_params=pltpu.CompilerParams(
            collective_id=0, has_side_effects=True, vmem_limit_bytes=56 << 20
        ),
    )(
        x_gate, x_key, x_value, conv_state, filter_taps,
        decay_rates.reshape(1, groups), skip_gain.reshape(1, chans),
        queries, stretch_keys, stretch_values, cache_keys, cache_values, prefix_len,
    )


def on_device(*arrays):
    rows, taps = arrays[0].shape[0], arrays[4].shape[1]
    if lax.axis_size("seq") == 4 and rows == taps == 128:
        return short_form(*arrays)
    return general_form(*arrays)


def solution(mesh):
    placed = (
        P(("parts", "seq"), "tp"),
        P(("parts", "seq"), "tp"),
        P(("parts", "seq"), "tp"),
        P("parts", "tp"),
        P("tp", None),
        P("tp"),
        P("tp"),
        P(("parts", "seq"), "tp"),
        P(("parts", "seq"), "tp"),
        P(("parts", "seq"), "tp"),
        P(("parts", "seq"), "tp"),
        P(("parts", "seq"), "tp"),
        P("parts"),
    )
    return jax.shard_map(
        on_device,
        mesh=mesh,
        in_specs=placed,
        out_specs=(P(("parts", "seq"), "tp"), P(("parts", "seq"), "tp")),
        check_vma=False,
    )
```

```python
import math

import jax
import jax.numpy as jnp
from jax import lax
from jax.experimental import pallas as pl
from jax.experimental.pallas import tpu as pltpu
from jax.sharding import PartitionSpec as P

HD = 128


far_position = 1 << 30


def shifted(value, axis, steps):
    count = lax.axis_size(axis)
    first, last = (max(0, -steps), min(count, count - steps))
    return lax.ppermute(value, axis, [(source, source + steps) for source in range(first, last)])


def general_form(
    x_gate,
    x_key,
    x_value,
    conv_state,
    filter_taps,
    decay_rates,
    skip_gain,
    queries,
    stretch_keys,
    stretch_values,
    cache_keys,
    cache_values,
    prefix_len,
):
    rows_dev = x_gate.shape[0]
    chans_dev = x_gate.shape[1]
    seq_index = lax.axis_index("seq")
    product_in = (x_key.astype(jnp.float32) * x_value.astype(jnp.float32)).astype(jnp.bfloat16)
    filter_reach = filter_taps.shape[1] - 1
    received = []
    taken = min(rows_dev, filter_reach)
    received.insert(0, shifted(product_in[rows_dev - taken :], "seq", 1))
    earlier = received[0]
    padded_state = jnp.concatenate(
        [conv_state, jnp.zeros((filter_reach, chans_dev), jnp.bfloat16)], axis=0
    )
    earlier = earlier + lax.dynamic_slice_in_dim(
        padded_state, seq_index * rows_dev, filter_reach, 0
    )
    extended = jnp.concatenate([earlier, product_in], axis=0)
    span_total = rows_dev + filter_reach
    tap_ramp = lax.iota(jnp.float32, filter_reach + 1)
    filters = (filter_taps * jnp.exp(-decay_rates[:, None] * tap_ramp[None, :])).astype(
        jnp.bfloat16
    )
    group_count = filters.shape[0]
    group_width = chans_dev // group_count
    skew_period = span_total + rows_dev - 1
    reversed_taps = jnp.concatenate(
        [filters[:, ::-1], jnp.zeros((group_count, skew_period - filter_reach - 1), jnp.bfloat16)],
        axis=1,
    )
    group_block = min(group_count, 16)
    conv_parts = []
    for first_group in range(0, group_count, group_block):
        taps_block = reversed_taps[first_group : first_group + group_block]
        toeplitz = jnp.tile(taps_block, (1, rows_dev + 1))[:, : rows_dev * (skew_period - 1)]
        toeplitz = toeplitz.reshape(group_block, rows_dev, skew_period - 1)[:, :, :span_total]
        columns = extended[:, first_group * group_width : (first_group + group_block) * group_width]
        columns = columns.reshape(span_total, group_block, group_width)
        conv_block = jnp.einsum(
            "gts,sgc->tgc", toeplitz, columns, preferred_element_type=jnp.float32
        )
        conv_parts.append(conv_block.reshape(rows_dev, group_block * group_width))
    filtered = jnp.concatenate(conv_parts, axis=1)
    hyena_out = (
        x_gate.astype(jnp.float32)
        * (filtered + skip_gain[None, :] * product_in.astype(jnp.float32))
    ).astype(jnp.bfloat16)
    head_count = queries.shape[1] // HD
    half_rows = rows_dev // 2
    scale_factor = 1.0 / math.sqrt(HD)
    half_ramp = lax.iota(jnp.int32, half_rows)
    second_base = seq_index * rows_dev + half_rows
    query_pos = jnp.stack([seq_index * rows_dev + half_ramp, second_base + half_ramp])
    query_heads = queries.reshape(2, half_rows, head_count, HD)
    limit_len = prefix_len[0]

    def consume(state, key_rows, value_rows, key_pos):
        row_total = key_rows.shape[0]
        if row_total <= 512:
            block_rows = row_total
            block_count = 1
        else:
            block_rows = 512
            block_count = -(-row_total // 512)
        key_blocks = key_rows.reshape(block_count, block_rows, head_count, HD)
        value_blocks = value_rows.reshape(block_count, block_rows, head_count, HD)
        pos_blocks = key_pos.reshape(block_count, block_rows)

        def one_block(block_step, inner):
            maxima, totals, sums = inner
            key_block = lax.dynamic_index_in_dim(key_blocks, block_step, 0, keepdims=False)
            value_block = lax.dynamic_index_in_dim(value_blocks, block_step, 0, keepdims=False)
            pos_block = lax.dynamic_index_in_dim(pos_blocks, block_step, 0, keepdims=False)
            for half_index in range(2):
                half_queries = query_heads[half_index]
                half_pos = query_pos[half_index]

                def update(parts):
                    run_max, run_total, run_sum = parts
                    scores = (
                        jnp.einsum(
                            "thd,shd->hts",
                            half_queries,
                            key_block,
                            preferred_element_type=jnp.float32,
                        )
                        * scale_factor
                    )
                    allowed = (pos_block[None, :] <= half_pos[:, None])[None]
                    scores = jnp.where(allowed, scores, -1e30)
                    new_max = jnp.maximum(run_max, jnp.max(scores, axis=2))
                    weights = jnp.where(allowed, jnp.exp(scores - new_max[:, :, None]), 0.0)
                    factor = jnp.exp(run_max - new_max)
                    new_total = run_total * factor + jnp.sum(weights, axis=2)
                    new_sum = run_sum * factor[:, :, None] + jnp.einsum(
                        "hts,shd->htd",
                        weights.astype(jnp.bfloat16),
                        value_block,
                        preferred_element_type=jnp.float32,
                    )
                    return (new_max, new_total, new_sum)

                def unchanged(parts):
                    return parts

                result = lax.cond(
                    jnp.min(pos_block) <= jnp.max(half_pos),
                    update,
                    unchanged,
                    (maxima[half_index], totals[half_index], sums[half_index]),
                )
                maxima = maxima.at[half_index].set(result[0])
                totals = totals.at[half_index].set(result[1])
                sums = sums.at[half_index].set(result[2])
            return (maxima, totals, sums)

        return lax.fori_loop(0, block_count, one_block, state)

    initial = (
        jnp.full((2, head_count, half_rows), -1e30, jnp.float32),
        jnp.zeros((2, head_count, half_rows), jnp.float32),
        jnp.zeros((2, head_count, half_rows, HD), jnp.float32),
    )
    cache_whole = (
        lax.all_gather(cache_keys, "seq", axis=0, tiled=True),
        lax.all_gather(cache_values, "seq", axis=0, tiled=True),
    )
    cache_ids = lax.iota(jnp.int32, cache_whole[0].shape[0])
    cache_pos = jnp.where(cache_ids < limit_len, -1, far_position)
    start_state = consume(initial, cache_whole[0], cache_whole[1], cache_pos)
    piece = (
        lax.all_gather(stretch_keys, "seq", axis=0, tiled=True),
        lax.all_gather(stretch_values, "seq", axis=0, tiled=True),
    )
    key_pos = lax.iota(jnp.int32, piece[0].shape[0])
    state = consume(start_state, piece[0], piece[1], key_pos)
    normalized = state[2] / state[1][:, :, :, None]
    result_rows = (
        normalized.transpose(0, 2, 1, 3).reshape(rows_dev, head_count * HD).astype(jnp.bfloat16)
    )
    return (hyena_out, result_rows)


MESH = pl.DeviceIdType.MESH
F32 = jnp.float32
BF16 = jnp.bfloat16


def remote(src, dst, send_sem, recv_sem, target):
    return pltpu.make_async_remote_copy(
        src_ref=src,
        dst_ref=dst,
        send_sem=send_sem,
        recv_sem=recv_sem,
        device_id={"seq": target},
        device_id_type=MESH,
    )


def short_kernel(
    x_gate, x_key, x_value, conv_state, filter_taps, decay_rates, skip_gain,
    queries, stretch_keys, stretch_values, cache_keys, cache_values, prefix_len,
    out_v, att_v,
    gate_v, key_v, value_v, state_v, taps_v, decay_v, skip_v, q_v, k_v, v_v,
    cache_k, cache_v, k_in, v_in, q_in, product_v, earlier_v, shifted_v,
    reversed_v, lower_v, upper_v, local_v,
    own_acc, own_stat, part_out, stat_out, part_in, stat_in,
    load_sem, send_sem, recv_sem, part_send, part_recv, cache_send, cache_recv,
):
    me = lax.axis_index("seq")
    rows, chans = gate_v.shape
    groups, taps = taps_v.shape
    width = chans // groups
    heads = q_v.shape[1] // HD
    scale_factor = 1.0 / math.sqrt(HD)

    loads = {}
    for at, (name, src, dst) in enumerate(
        [
            ("key", x_key, key_v),
            ("value", x_value, value_v),
            ("taps", filter_taps, taps_v),
            ("decay", decay_rates, decay_v),
            ("q", queries, q_v),
            ("k", stretch_keys, k_v),
            ("v", stretch_values, v_v),
            ("skip", skip_gain, skip_v),
            ("gate", x_gate, gate_v),
            ("state", conv_state, state_v),
            ("ck", cache_keys, cache_k.at[me]),
            ("cv", cache_values, cache_v.at[me]),
        ]
    ):
        loads[name] = pltpu.make_async_copy(src, dst, load_sem.at[at])
        loads[name].start()

    barrier = pltpu.get_barrier_semaphore()
    for step in range(1, 4):
        pl.semaphore_signal(
            barrier, inc=1, device_id={"seq": lax.rem(me + step, 4)}, device_id_type=MESH
        )
    pl.semaphore_wait(barrier, 3)

    send_k = remote(stretch_keys, k_in, send_sem.at[0], recv_sem.at[0], 1)
    send_v = remote(stretch_values, v_in, send_sem.at[1], recv_sem.at[1], 1)
    send_q2 = remote(queries, q_in.at[0], send_sem.at[2], recv_sem.at[2], 1)
    send_q3 = remote(queries, q_in.at[1], send_sem.at[3], recv_sem.at[3], 1)
    send_q3_near = remote(queries, q_in.at[1], send_sem.at[2], recv_sem.at[3], 2)
    send_product = [
        remote(
            product_v.at[:, pl.ds(half * chans // 2, chans // 2)],
            earlier_v.at[:, pl.ds(half * chans // 2, chans // 2)],
            send_sem.at[4 + half], recv_sem.at[4 + half], lax.rem(me + 1, 4),
        )
        for half in range(2)
    ]

    def send_part(slot, landing, head, target):
        return [
            remote(
                src.at[slot, head], dst.at[landing, head],
                part_send.at[which, slot, head], part_recv.at[which, landing, head], target,
            )
            for which, (src, dst) in enumerate([(part_out, part_in), (stat_out, stat_in)])
        ]

    @pl.when(me == 0)
    def _():
        send_k.start()
        send_v.start()

    @pl.when(me == 2)
    def _():
        send_q2.start()

    @pl.when(me == 3)
    def _():
        send_q3.start()
        send_q3_near.start()

    cache_copies = []
    for step in range(1, 4):
        target = lax.rem(me + step, 4)
        for which, (src, dst) in enumerate(
            [(cache_keys, cache_k), (cache_values, cache_v)]
        ):
            copy = remote(
                src, dst.at[me], cache_send.at[which, step - 1], cache_recv.at[which, me], target
            )
            copy.start()
            cache_copies.append(copy)

    loads["key"].wait()
    loads["value"].wait()
    product_v[...] = (key_v[...].astype(F32) * value_v[...].astype(F32)).astype(BF16)

    @pl.when((me > 0) & (me < 3))
    def _():
        for copy in send_product:
            copy.start()

    loads["taps"].wait()
    loads["decay"].wait()
    row_id = lax.broadcasted_iota(jnp.int32, (groups, groups), 0)
    col_id = lax.broadcasted_iota(jnp.int32, (groups, groups), 1)
    rates = jnp.sum(
        jnp.where(row_id == col_id, decay_v[...], 0.0), axis=1, keepdims=True
    )
    ramp = lax.broadcasted_iota(jnp.int32, (groups, taps), 1).astype(F32)
    filters = (taps_v[...] * jnp.exp(-rates * ramp)).astype(BF16)
    from_id = lax.broadcasted_iota(jnp.int32, (taps, taps), 0)
    to_id = lax.broadcasted_iota(jnp.int32, (taps, taps), 1)
    total_id = from_id + to_id
    flip = jnp.where((total_id == 0) | (total_id == taps), 1.0, 0.0).astype(BF16)
    reversed_v[...] = jnp.dot(filters, flip, preferred_element_type=F32)
    below = to_id <= from_id

    def build(pair, carry):
        for half in range(2):
            row = reversed_v[pl.ds(pair * 2 + half, 1), :]
            circ = pltpu.roll(
                jnp.broadcast_to(row, (rows, taps)), 0, 1, stride=1, stride_axis=0
            )
            lanes = pl.ds(half * taps, taps)
            lower_v[pair, :, lanes] = jnp.where(below, circ, 0.0).astype(BF16)
            upper_v[pair, :, lanes] = jnp.where(below, 0.0, circ).astype(BF16)
        return carry

    lax.fori_loop(0, groups // 2, build, 0)

    lane = lax.broadcasted_iota(jnp.int32, (1, 128), 1)
    odd_lane = lax.rem(lane // width, 2) == 1
    odd = jnp.where(odd_lane, 1.0, 0.0).astype(BF16)
    even = jnp.where(odd_lane, 0.0, 1.0).astype(BF16)
    pair_of = lax.broadcasted_iota(jnp.int32, (rows, 128), 1) // (2 * width)
    pairs = 128 // (2 * width)

    def filtered(matrix_ref, block, tile):
        stacked = jnp.concatenate([block * even, block * odd], axis=0)
        total = None
        for at in range(pairs):
            term = jnp.dot(
                matrix_ref[tile * pairs + at], stacked, preferred_element_type=F32
            )
            total = term if total is None else jnp.where(pair_of == at, term, total)
        return total

    loads["skip"].wait()
    for tile in range(chans // 128):
        cols = slice(tile * 128, (tile + 1) * 128)
        block = product_v[:, cols]
        local_v[:, cols] = filtered(lower_v, block, tile) + skip_v[:, cols] * block.astype(F32)

    @pl.when(me == 0)
    def _():
        send_k.wait_send()
        send_v.wait_send()
        for copy in send_product:
            copy.start()

    loads["q"].wait()
    loads["k"].wait()
    loads["v"].wait()
    loads["ck"].wait()
    loads["cv"].wait()
    for step in range(1, 4):
        source = lax.rem(me + step, 4)
        for which, (src, dst) in enumerate(
            [(cache_keys, cache_k), (cache_values, cache_v)]
        ):
            remote(
                src, dst.at[source], cache_send.at[which, step - 1],
                cache_recv.at[which, source], source,
            ).wait_recv()

    def joined(ref, cols):
        return jnp.concatenate(
            [ref[at, :, cols].astype(F32) for at in range(4)], axis=0
        ).astype(BF16)

    cache_rows = 4 * cache_k.shape[1]
    causal = to_id >= from_id
    in_prefix = (
        lax.broadcasted_iota(jnp.int32, (cache_rows, rows), 0) < prefix_len[0]
    )

    def attend(query, blocks):
        scores = []
        for key, value, allowed in blocks:
            score = (
                lax.dot_general(
                    key, query, (((1,), (1,)), ((), ())), preferred_element_type=F32
                )
                * scale_factor
            )
            if allowed is not None:
                score = jnp.where(allowed, score, -1e30)
            scores.append(score)
        top = jnp.max(scores[0], axis=0, keepdims=True)
        for score in scores[1:]:
            top = jnp.maximum(top, jnp.max(score, axis=0, keepdims=True))
        total, mixed = 0.0, 0.0
        for score, (key, value, allowed) in zip(scores, blocks):
            weight = jnp.exp(score - top)
            if allowed is not None:
                weight = jnp.where(allowed, weight, 0.0)
            total = total + jnp.sum(weight, axis=0, keepdims=True)
            mixed = mixed + lax.dot_general(
                value, weight.astype(BF16), (((0,), (0,)), ((), ())),
                preferred_element_type=F32,
            )
        return top, total, mixed

    def head_cols(head):
        return slice(head * HD, (head + 1) * HD)

    def own_blocks(head):
        cols = head_cols(head)
        return [
            (joined(cache_k, cols), joined(cache_v, cols), in_prefix),
            (k_v[:, cols], v_v[:, cols], causal),
        ]

    def keep(head, result):
        own_stat[head : head + 1, :] = result[0]
        own_stat[heads + head : heads + head + 1, :] = result[1]
        own_acc[head] = result[2]

    def give(slot, head, result):
        stat_out[slot, head, 0:1, :] = result[0]
        stat_out[slot, head, 1:2, :] = result[1]
        part_out[slot, head] = (result[2] / result[1]).astype(BF16)

    @pl.when(me != 1)
    def _():
        for head in range(heads):
            keep(head, attend(q_v[:, head_cols(head)], own_blocks(head)))

    @pl.when(me == 1)
    def _():
        send_k.wait_recv()
        send_v.wait_recv()

        def shared_blocks(cols):
            return [
                (k_in[:, cols], v_in[:, cols], None),
                (k_v[:, cols], v_v[:, cols], None),
            ]

        for slot, arrival, target in ((1, send_q3, 3), (0, send_q2, 2)):
            arrival.wait_recv()
            for head in range(heads):
                cols = head_cols(head)
                give(slot, head, attend(q_in[slot, :, cols], shared_blocks(cols)))
                for copy in send_part(slot, 0, head, target):
                    copy.start()
        for head in range(heads):
            cols = head_cols(head)
            keep(
                head,
                attend(
                    q_v[:, cols], own_blocks(head) + [(k_in[:, cols], v_in[:, cols], None)]
                ),
            )

    @pl.when(me == 2)
    def _():
        send_q3_near.wait_recv()
        for head in range(heads):
            cols = head_cols(head)
            give(1, head, attend(q_in[1, :, cols], [(k_v[:, cols], v_v[:, cols], None)]))
            for copy in send_part(1, 1, head, 3):
                copy.start()

    loads["state"].wait()

    @pl.when(me == 0)
    def _():
        shifted_v[0:1, :] = jnp.zeros((1, chans), F32)
        shifted_v[pl.ds(1, rows - 1), :] = state_v[...].astype(F32)
        earlier_v[...] = shifted_v[...].astype(BF16)

    loads["gate"].wait()
    tiles = chans // 128
    for tile in range(tiles):
        if tile % (tiles // 2) == 0:

            @pl.when(me > 0)
            def _():
                send_product[tile // (tiles // 2)].wait_recv()

        cols = slice(tile * 128, (tile + 1) * 128)
        whole = local_v[:, cols] + filtered(upper_v, earlier_v[:, cols], tile)
        out_v[:, cols] = (gate_v[:, cols].astype(F32) * whole).astype(BF16)

    def finish(slots):
        for head in range(heads):
            for slot in slots:
                for copy in send_part(1, slot, head, 1):
                    copy.wait_recv()
            top = own_stat[head : head + 1, :]
            tops = [stat_in[slot, head, 0:1, :] for slot in slots]
            best = top
            for other in tops:
                best = jnp.maximum(best, other)
            share = jnp.exp(top - best)
            total = own_stat[heads + head : heads + head + 1, :] * share
            mixed = own_acc[head] * share
            for slot, other in zip(slots, tops):
                share = stat_in[slot, head, 1:2, :] * jnp.exp(other - best)
                total = total + share
                mixed = mixed + part_in[slot, head].astype(F32) * share
            att_v[:, head_cols(head)] = (mixed / total).T.astype(BF16)

    @pl.when(me < 2)
    def _():
        finish([])

    @pl.when(me == 2)
    def _():
        finish([0])

    @pl.when(me == 3)
    def _():
        finish([1, 0])

    for copy in cache_copies:
        copy.wait_send()

    @pl.when(me < 3)
    def _():
        for copy in send_product:
            copy.wait_send()

    @pl.when(me == 1)
    def _():
        for head in range(heads):
            for copy in send_part(1, 0, head, 3) + send_part(0, 0, head, 2):
                copy.wait_send()

    @pl.when(me == 2)
    def _():
        send_q2.wait_send()
        for head in range(heads):
            for copy in send_part(1, 1, head, 3):
                copy.wait_send()

    @pl.when(me == 3)
    def _():
        send_q3.wait_send()
        send_q3_near.wait_send()


def short_form(
    x_gate, x_key, x_value, conv_state, filter_taps, decay_rates, skip_gain,
    queries, stretch_keys, stretch_values, cache_keys, cache_values, prefix_len,
):
    rows, chans = x_gate.shape
    groups, taps = filter_taps.shape
    across = queries.shape[1]
    heads = across // HD
    cache_rows = cache_keys.shape[0]
    any_spec = pl.BlockSpec(memory_space=pltpu.HBM)
    dma = pltpu.SemaphoreType.DMA
    vm = pltpu.VMEM
    return pl.pallas_call(
        short_kernel,
        out_shape=(
            jax.ShapeDtypeStruct((rows, chans), BF16),
            jax.ShapeDtypeStruct((rows, across), BF16),
        ),
        in_specs=[any_spec] * 12 + [pl.BlockSpec(memory_space=pltpu.SMEM)],
        out_specs=(pl.BlockSpec(memory_space=pltpu.VMEM),) * 2,
        scratch_shapes=[
            vm((rows, chans), BF16),
            vm((rows, chans), BF16),
            vm((rows, chans), BF16),
            vm((rows - 1, chans), BF16),
            vm((groups, taps), F32),
            vm((1, groups), F32),
            vm((1, chans), F32),
            vm((rows, across), BF16),
            vm((rows, across), BF16),
            vm((rows, across), BF16),
            vm((4, cache_rows, across), BF16),
            vm((4, cache_rows, across), BF16),
            vm((rows, across), BF16),
            vm((rows, across), BF16),
            vm((2, rows, across), BF16),
            vm((rows, chans), BF16),
            vm((rows, chans), BF16),
            vm((rows, chans), F32),
            vm((groups, taps), F32),
            vm((groups // 2, rows, 2 * taps), BF16),
            vm((groups // 2, rows, 2 * taps), BF16),
            vm((rows, chans), F32),
            vm((heads, HD, rows), F32),
            vm((2 * heads, rows), F32),
            vm((2, heads, HD, rows), BF16),
            vm((2, heads, 2, rows), F32),
            vm((2, heads, HD, rows), BF16),
            vm((2, heads, 2, rows), F32),
            dma((12,)),
            dma((6,)),
            dma((6,)),
            dma((2, 2, heads)),
            dma((2, 2, heads)),
            dma((2, 3)),
            dma((2, 4)),
        ],
        compiler_params=pltpu.CompilerParams(
            collective_id=0, has_side_effects=True, vmem_limit_bytes=40 << 20
        ),
    )(
        *(
            pltpu.with_memory_space_constraint(array, pltpu.HBM)
            for array in (
                x_gate, x_key, x_value, conv_state, filter_taps,
                decay_rates.reshape(1, groups), skip_gain.reshape(1, chans),
                queries, stretch_keys, stretch_values, cache_keys, cache_values,
            )
        ),
        prefix_len,
    )


def on_device(*arrays):
    rows, taps = arrays[0].shape[0], arrays[4].shape[1]
    if lax.axis_size("seq") == 4 and rows == taps == 128:
        return short_form(*arrays)
    return general_form(*arrays)


def solution(mesh):
    placed = (
        P(("parts", "seq"), "tp"),
        P(("parts", "seq"), "tp"),
        P(("parts", "seq"), "tp"),
        P("parts", "tp"),
        P("tp", None),
        P("tp"),
        P("tp"),
        P(("parts", "seq"), "tp"),
        P(("parts", "seq"), "tp"),
        P(("parts", "seq"), "tp"),
        P(("parts", "seq"), "tp"),
        P(("parts", "seq"), "tp"),
        P("parts"),
    )
    return jax.shard_map(
        on_device,
        mesh=mesh,
        in_specs=placed,
        out_specs=(P(("parts", "seq"), "tp"), P(("parts", "seq"), "tp")),
        check_vma=False,
    )
```

```python
import math

import jax
import jax.numpy as jnp
from jax import lax
from jax.experimental import pallas as pl
from jax.experimental.pallas import tpu as pltpu
from jax.sharding import PartitionSpec as P

HD = 128


far_position = 1 << 30


def shifted(value, axis, steps):
    count = lax.axis_size(axis)
    first, last = (max(0, -steps), min(count, count - steps))
    return lax.ppermute(value, axis, [(source, source + steps) for source in range(first, last)])


def general_form(
    x_gate,
    x_key,
    x_value,
    conv_state,
    filter_taps,
    decay_rates,
    skip_gain,
    queries,
    stretch_keys,
    stretch_values,
    cache_keys,
    cache_values,
    prefix_len,
):
    rows_dev = x_gate.shape[0]
    chans_dev = x_gate.shape[1]
    seq_index = lax.axis_index("seq")
    product_in = (x_key.astype(jnp.float32) * x_value.astype(jnp.float32)).astype(jnp.bfloat16)
    filter_reach = filter_taps.shape[1] - 1
    received = []
    taken = min(rows_dev, filter_reach)
    received.insert(0, shifted(product_in[rows_dev - taken :], "seq", 1))
    earlier = received[0]
    padded_state = jnp.concatenate(
        [conv_state, jnp.zeros((filter_reach, chans_dev), jnp.bfloat16)], axis=0
    )
    earlier = earlier + lax.dynamic_slice_in_dim(
        padded_state, seq_index * rows_dev, filter_reach, 0
    )
    extended = jnp.concatenate([earlier, product_in], axis=0)
    span_total = rows_dev + filter_reach
    tap_ramp = lax.iota(jnp.float32, filter_reach + 1)
    filters = (filter_taps * jnp.exp(-decay_rates[:, None] * tap_ramp[None, :])).astype(
        jnp.bfloat16
    )
    group_count = filters.shape[0]
    group_width = chans_dev // group_count
    skew_period = span_total + rows_dev - 1
    reversed_taps = jnp.concatenate(
        [filters[:, ::-1], jnp.zeros((group_count, skew_period - filter_reach - 1), jnp.bfloat16)],
        axis=1,
    )
    group_block = min(group_count, 16)
    conv_parts = []
    for first_group in range(0, group_count, group_block):
        taps_block = reversed_taps[first_group : first_group + group_block]
        toeplitz = jnp.tile(taps_block, (1, rows_dev + 1))[:, : rows_dev * (skew_period - 1)]
        toeplitz = toeplitz.reshape(group_block, rows_dev, skew_period - 1)[:, :, :span_total]
        columns = extended[:, first_group * group_width : (first_group + group_block) * group_width]
        columns = columns.reshape(span_total, group_block, group_width)
        conv_block = jnp.einsum(
            "gts,sgc->tgc", toeplitz, columns, preferred_element_type=jnp.float32
        )
        conv_parts.append(conv_block.reshape(rows_dev, group_block * group_width))
    filtered = jnp.concatenate(conv_parts, axis=1)
    hyena_out = (
        x_gate.astype(jnp.float32)
        * (filtered + skip_gain[None, :] * product_in.astype(jnp.float32))
    ).astype(jnp.bfloat16)
    head_count = queries.shape[1] // HD
    half_rows = rows_dev // 2
    scale_factor = 1.0 / math.sqrt(HD)
    half_ramp = lax.iota(jnp.int32, half_rows)
    second_base = seq_index * rows_dev + half_rows
    query_pos = jnp.stack([seq_index * rows_dev + half_ramp, second_base + half_ramp])
    query_heads = queries.reshape(2, half_rows, head_count, HD)
    limit_len = prefix_len[0]

    def consume(state, key_rows, value_rows, key_pos):
        row_total = key_rows.shape[0]
        if row_total <= 512:
            block_rows = row_total
            block_count = 1
        else:
            block_rows = 512
            block_count = -(-row_total // 512)
        key_blocks = key_rows.reshape(block_count, block_rows, head_count, HD)
        value_blocks = value_rows.reshape(block_count, block_rows, head_count, HD)
        pos_blocks = key_pos.reshape(block_count, block_rows)

        def one_block(block_step, inner):
            maxima, totals, sums = inner
            key_block = lax.dynamic_index_in_dim(key_blocks, block_step, 0, keepdims=False)
            value_block = lax.dynamic_index_in_dim(value_blocks, block_step, 0, keepdims=False)
            pos_block = lax.dynamic_index_in_dim(pos_blocks, block_step, 0, keepdims=False)
            for half_index in range(2):
                half_queries = query_heads[half_index]
                half_pos = query_pos[half_index]

                def update(parts):
                    run_max, run_total, run_sum = parts
                    scores = (
                        jnp.einsum(
                            "thd,shd->hts",
                            half_queries,
                            key_block,
                            preferred_element_type=jnp.float32,
                        )
                        * scale_factor
                    )
                    allowed = (pos_block[None, :] <= half_pos[:, None])[None]
                    scores = jnp.where(allowed, scores, -1e30)
                    new_max = jnp.maximum(run_max, jnp.max(scores, axis=2))
                    weights = jnp.where(allowed, jnp.exp(scores - new_max[:, :, None]), 0.0)
                    factor = jnp.exp(run_max - new_max)
                    new_total = run_total * factor + jnp.sum(weights, axis=2)
                    new_sum = run_sum * factor[:, :, None] + jnp.einsum(
                        "hts,shd->htd",
                        weights.astype(jnp.bfloat16),
                        value_block,
                        preferred_element_type=jnp.float32,
                    )
                    return (new_max, new_total, new_sum)

                def unchanged(parts):
                    return parts

                result = lax.cond(
                    jnp.min(pos_block) <= jnp.max(half_pos),
                    update,
                    unchanged,
                    (maxima[half_index], totals[half_index], sums[half_index]),
                )
                maxima = maxima.at[half_index].set(result[0])
                totals = totals.at[half_index].set(result[1])
                sums = sums.at[half_index].set(result[2])
            return (maxima, totals, sums)

        return lax.fori_loop(0, block_count, one_block, state)

    initial = (
        jnp.full((2, head_count, half_rows), -1e30, jnp.float32),
        jnp.zeros((2, head_count, half_rows), jnp.float32),
        jnp.zeros((2, head_count, half_rows, HD), jnp.float32),
    )
    cache_whole = (
        lax.all_gather(cache_keys, "seq", axis=0, tiled=True),
        lax.all_gather(cache_values, "seq", axis=0, tiled=True),
    )
    cache_ids = lax.iota(jnp.int32, cache_whole[0].shape[0])
    cache_pos = jnp.where(cache_ids < limit_len, -1, far_position)
    start_state = consume(initial, cache_whole[0], cache_whole[1], cache_pos)
    piece = (
        lax.all_gather(stretch_keys, "seq", axis=0, tiled=True),
        lax.all_gather(stretch_values, "seq", axis=0, tiled=True),
    )
    key_pos = lax.iota(jnp.int32, piece[0].shape[0])
    state = consume(start_state, piece[0], piece[1], key_pos)
    normalized = state[2] / state[1][:, :, :, None]
    result_rows = (
        normalized.transpose(0, 2, 1, 3).reshape(rows_dev, head_count * HD).astype(jnp.bfloat16)
    )
    return (hyena_out, result_rows)


MESH = pl.DeviceIdType.MESH
F32 = jnp.float32
BF16 = jnp.bfloat16


def remote(src, dst, send_sem, recv_sem, target):
    return pltpu.make_async_remote_copy(
        src_ref=src,
        dst_ref=dst,
        send_sem=send_sem,
        recv_sem=recv_sem,
        device_id={"seq": target},
        device_id_type=MESH,
    )


def short_kernel(
    x_gate, x_key, x_value, conv_state, filter_taps, decay_rates, skip_gain,
    queries, stretch_keys, stretch_values, cache_keys, cache_values, prefix_len,
    out_v, att_v,
    gate_v, key_v, value_v, state_v, taps_v, decay_v, skip_v, q_v, k_v, v_v,
    cache_k, cache_v, k_in, v_in, q_in, product_v, earlier_v, shifted_v,
    reversed_v, lower_v, upper_v, local_v,
    own_acc, own_stat, part_out, stat_out, part_in, stat_in,
    load_sem, send_sem, recv_sem, part_send, part_recv, cache_send, cache_recv,
):
    me = lax.axis_index("seq")
    rows, chans = gate_v.shape
    groups, taps = taps_v.shape
    width = chans // groups
    heads = q_v.shape[1] // HD
    scale_factor = 1.0 / math.sqrt(HD)

    loads = {}
    for at, (name, src, dst) in enumerate(
        [
            ("key", x_key, key_v),
            ("value", x_value, value_v),
            ("taps", filter_taps, taps_v),
            ("decay", decay_rates, decay_v),
            ("q", queries, q_v),
            ("k", stretch_keys, k_v),
            ("v", stretch_values, v_v),
            ("skip", skip_gain, skip_v),
            ("gate", x_gate, gate_v),
            ("state", conv_state, state_v),
            ("ck", cache_keys, cache_k.at[me]),
            ("cv", cache_values, cache_v.at[me]),
        ]
    ):
        loads[name] = pltpu.make_async_copy(src, dst, load_sem.at[at])
        loads[name].start()

    barrier = pltpu.get_barrier_semaphore()
    for step in range(1, 4):
        pl.semaphore_signal(
            barrier, inc=1, device_id={"seq": lax.rem(me + step, 4)}, device_id_type=MESH
        )
    pl.semaphore_wait(barrier, 3)

    send_k = remote(stretch_keys, k_in, send_sem.at[0], recv_sem.at[0], 1)
    send_v = remote(stretch_values, v_in, send_sem.at[1], recv_sem.at[1], 1)
    send_q2 = remote(queries, q_in.at[0], send_sem.at[2], recv_sem.at[2], 1)
    send_q3 = remote(queries, q_in.at[1], send_sem.at[3], recv_sem.at[3], 1)
    send_q3_near = remote(queries, q_in.at[1], send_sem.at[2], recv_sem.at[3], 2)
    send_product = [
        remote(
            product_v.at[:, pl.ds(half * chans // 2, chans // 2)],
            earlier_v.at[:, pl.ds(half * chans // 2, chans // 2)],
            send_sem.at[4 + half], recv_sem.at[4 + half], lax.rem(me + 1, 4),
        )
        for half in range(2)
    ]

    def send_part(slot, landing, head, target):
        return [
            remote(
                src.at[slot, head], dst.at[landing, head],
                part_send.at[which, slot, head], part_recv.at[which, landing, head], target,
            )
            for which, (src, dst) in enumerate([(part_out, part_in), (stat_out, stat_in)])
        ]

    @pl.when(me == 0)
    def _():
        send_k.start()
        send_v.start()

    @pl.when(me == 2)
    def _():
        send_q2.start()

    @pl.when(me == 3)
    def _():
        send_q3.start()
        send_q3_near.start()

    cache_copies = []
    for step in range(1, 4):
        target = lax.rem(me + step, 4)
        for which, (src, dst) in enumerate(
            [(cache_keys, cache_k), (cache_values, cache_v)]
        ):
            copy = remote(
                src, dst.at[me], cache_send.at[which, step - 1], cache_recv.at[which, me], target
            )
            copy.start()
            cache_copies.append(copy)

    loads["key"].wait()
    loads["value"].wait()
    product_v[...] = (key_v[...].astype(F32) * value_v[...].astype(F32)).astype(BF16)

    @pl.when((me > 0) & (me < 3))
    def _():
        for copy in send_product:
            copy.start()

    loads["taps"].wait()
    loads["decay"].wait()
    row_id = lax.broadcasted_iota(jnp.int32, (groups, groups), 0)
    col_id = lax.broadcasted_iota(jnp.int32, (groups, groups), 1)
    rates = jnp.sum(
        jnp.where(row_id == col_id, decay_v[...], 0.0), axis=1, keepdims=True
    )
    ramp = lax.broadcasted_iota(jnp.int32, (groups, taps), 1).astype(F32)
    filters = (taps_v[...] * jnp.exp(-rates * ramp)).astype(BF16)
    from_id = lax.broadcasted_iota(jnp.int32, (taps, taps), 0)
    to_id = lax.broadcasted_iota(jnp.int32, (taps, taps), 1)
    total_id = from_id + to_id
    flip = jnp.where((total_id == 0) | (total_id == taps), 1.0, 0.0).astype(BF16)
    reversed_v[...] = jnp.dot(filters, flip, preferred_element_type=F32)
    below = to_id <= from_id

    def build(pair, carry):
        for half in range(2):
            row = reversed_v[pl.ds(pair * 2 + half, 1), :]
            circ = pltpu.roll(
                jnp.broadcast_to(row, (rows, taps)), 0, 1, stride=1, stride_axis=0
            )
            lanes = pl.ds(half * taps, taps)
            lower_v[pair, :, lanes] = jnp.where(below, circ, 0.0).astype(BF16)
            upper_v[pair, :, lanes] = jnp.where(below, 0.0, circ).astype(BF16)
        return carry

    lax.fori_loop(0, groups // 2, build, 0)

    lane = lax.broadcasted_iota(jnp.int32, (1, 128), 1)
    odd_lane = lax.rem(lane // width, 2) == 1
    odd = jnp.where(odd_lane, 1.0, 0.0).astype(BF16)
    even = jnp.where(odd_lane, 0.0, 1.0).astype(BF16)
    pair_of = lax.broadcasted_iota(jnp.int32, (rows, 128), 1) // (2 * width)
    pairs = 128 // (2 * width)

    def filtered(matrix_ref, block, tile):
        stacked = jnp.concatenate([block * even, block * odd], axis=0)
        total = None
        for at in range(pairs):
            term = jnp.dot(
                matrix_ref[tile * pairs + at], stacked, preferred_element_type=F32
            )
            total = term if total is None else jnp.where(pair_of == at, term, total)
        return total

    loads["skip"].wait()
    for tile in range(chans // 128):
        cols = slice(tile * 128, (tile + 1) * 128)
        block = product_v[:, cols]
        local_v[:, cols] = filtered(lower_v, block, tile) + skip_v[:, cols] * block.astype(F32)

    @pl.when(me == 0)
    def _():
        send_k.wait_send()
        send_v.wait_send()
        for copy in send_product:
            copy.start()

    loads["q"].wait()
    loads["k"].wait()
    loads["v"].wait()
    loads["ck"].wait()
    loads["cv"].wait()
    for step in range(1, 4):
        source = lax.rem(me + step, 4)
        for which, (src, dst) in enumerate(
            [(cache_keys, cache_k), (cache_values, cache_v)]
        ):
            remote(
                src, dst.at[source], cache_send.at[which, step - 1],
                cache_recv.at[which, source], source,
            ).wait_recv()

    def joined(ref, cols):
        return jnp.concatenate(
            [ref[at, :, cols].astype(F32) for at in range(4)], axis=0
        ).astype(BF16)

    cache_rows = 4 * cache_k.shape[1]
    causal = to_id >= from_id
    in_prefix = (
        lax.broadcasted_iota(jnp.int32, (cache_rows, rows), 0) < prefix_len[0]
    )

    def attend(query, blocks):
        scores = []
        for key, value, allowed in blocks:
            score = (
                lax.dot_general(
                    key, query, (((1,), (1,)), ((), ())), preferred_element_type=F32
                )
                * scale_factor
            )
            if allowed is not None:
                score = jnp.where(allowed, score, -1e30)
            scores.append(score)
        top = jnp.max(scores[0], axis=0, keepdims=True)
        for score in scores[1:]:
            top = jnp.maximum(top, jnp.max(score, axis=0, keepdims=True))
        total, mixed = 0.0, 0.0
        for score, (key, value, allowed) in zip(scores, blocks):
            weight = jnp.exp(score - top)
            if allowed is not None:
                weight = jnp.where(allowed, weight, 0.0)
            total = total + jnp.sum(weight, axis=0, keepdims=True)
            mixed = mixed + lax.dot_general(
                value, weight.astype(BF16), (((0,), (0,)), ((), ())),
                preferred_element_type=F32,
            )
        return top, total, mixed

    def head_cols(head):
        return slice(head * HD, (head + 1) * HD)

    def own_blocks(head):
        cols = head_cols(head)
        return [
            (joined(cache_k, cols), joined(cache_v, cols), in_prefix),
            (k_v[:, cols], v_v[:, cols], causal),
        ]

    def keep(head, result):
        own_stat[head : head + 1, :] = result[0]
        own_stat[heads + head : heads + head + 1, :] = result[1]
        own_acc[head] = result[2]

    def give(slot, head, result):
        stat_out[slot, head, 0:1, :] = result[0]
        stat_out[slot, head, 1:2, :] = result[1]
        part_out[slot, head] = (result[2] / result[1]).astype(BF16)

    @pl.when(me != 1)
    def _():
        for head in range(heads):
            keep(head, attend(q_v[:, head_cols(head)], own_blocks(head)))

    @pl.when(me == 1)
    def _():
        send_k.wait_recv()
        send_v.wait_recv()

        def shared_blocks(cols):
            return [
                (k_in[:, cols], v_in[:, cols], None),
                (k_v[:, cols], v_v[:, cols], None),
            ]

        for slot, arrival, target in ((1, send_q3, 3), (0, send_q2, 2)):
            arrival.wait_recv()
            for head in range(heads):
                cols = head_cols(head)
                give(slot, head, attend(q_in[slot, :, cols], shared_blocks(cols)))
                for copy in send_part(slot, 0, head, target):
                    copy.start()
        for head in range(heads):
            cols = head_cols(head)
            keep(
                head,
                attend(
                    q_v[:, cols], own_blocks(head) + [(k_in[:, cols], v_in[:, cols], None)]
                ),
            )

    @pl.when(me == 2)
    def _():
        send_q3_near.wait_recv()
        for head in range(heads):
            cols = head_cols(head)
            give(1, head, attend(q_in[1, :, cols], [(k_v[:, cols], v_v[:, cols], None)]))
            for copy in send_part(1, 1, head, 3):
                copy.start()

    loads["state"].wait()

    @pl.when(me == 0)
    def _():
        shifted_v[0:1, :] = jnp.zeros((1, chans), F32)
        shifted_v[pl.ds(1, rows - 1), :] = state_v[...].astype(F32)
        earlier_v[...] = shifted_v[...].astype(BF16)

    loads["gate"].wait()
    tiles = chans // 128
    for tile in range(tiles):
        if tile % (tiles // 2) == 0:

            @pl.when(me > 0)
            def _():
                send_product[tile // (tiles // 2)].wait_recv()

        cols = slice(tile * 128, (tile + 1) * 128)
        whole = local_v[:, cols] + filtered(upper_v, earlier_v[:, cols], tile)
        out_v[:, cols] = (gate_v[:, cols].astype(F32) * whole).astype(BF16)

    def finish(slots):
        for head in range(heads):
            for slot in slots:
                for copy in send_part(1, slot, head, 1):
                    copy.wait_recv()
            top = own_stat[head : head + 1, :]
            tops = [stat_in[slot, head, 0:1, :] for slot in slots]
            best = top
            for other in tops:
                best = jnp.maximum(best, other)
            share = jnp.exp(top - best)
            total = own_stat[heads + head : heads + head + 1, :] * share
            mixed = own_acc[head] * share
            for slot, other in zip(slots, tops):
                share = stat_in[slot, head, 1:2, :] * jnp.exp(other - best)
                total = total + share
                mixed = mixed + part_in[slot, head].astype(F32) * share
            att_v[:, head_cols(head)] = (mixed / total).T.astype(BF16)

    @pl.when(me < 2)
    def _():
        finish([])

    @pl.when(me == 2)
    def _():
        finish([0])

    @pl.when(me == 3)
    def _():
        finish([1, 0])

    for copy in cache_copies:
        copy.wait_send()

    @pl.when(me < 3)
    def _():
        for copy in send_product:
            copy.wait_send()

    @pl.when(me == 1)
    def _():
        for head in range(heads):
            for copy in send_part(1, 0, head, 3) + send_part(0, 0, head, 2):
                copy.wait_send()

    @pl.when(me == 2)
    def _():
        send_q2.wait_send()
        for head in range(heads):
            for copy in send_part(1, 1, head, 3):
                copy.wait_send()

    @pl.when(me == 3)
    def _():
        send_q3.wait_send()
        send_q3_near.wait_send()


def store_kernel(hyena_in, attention_in, hyena_out, attention_out, sem):
    copies = [
        pltpu.make_async_copy(hyena_in, hyena_out, sem.at[0]),
        pltpu.make_async_copy(attention_in, attention_out, sem.at[1]),
    ]
    for copy in copies:
        copy.start()
    for copy in copies:
        copy.wait()


def short_form(
    x_gate, x_key, x_value, conv_state, filter_taps, decay_rates, skip_gain,
    queries, stretch_keys, stretch_values, cache_keys, cache_values, prefix_len,
):
    rows, chans = x_gate.shape
    groups, taps = filter_taps.shape
    across = queries.shape[1]
    heads = across // HD
    cache_rows = cache_keys.shape[0]
    any_spec = pl.BlockSpec(memory_space=pltpu.HBM)
    dma = pltpu.SemaphoreType.DMA
    vm = pltpu.VMEM
    held = pl.pallas_call(
        short_kernel,
        out_shape=(
            pltpu.VMEM((rows, chans), BF16),
            pltpu.VMEM((rows, across), BF16),
        ),
        in_specs=[any_spec] * 12 + [pl.BlockSpec(memory_space=pltpu.SMEM)],
        out_specs=(pl.BlockSpec(memory_space=pltpu.VMEM),) * 2,
        scratch_shapes=[
            vm((rows, chans), BF16),
            vm((rows, chans), BF16),
            vm((rows, chans), BF16),
            vm((rows - 1, chans), BF16),
            vm((groups, taps), F32),
            vm((1, groups), F32),
            vm((1, chans), F32),
            vm((rows, across), BF16),
            vm((rows, across), BF16),
            vm((rows, across), BF16),
            vm((4, cache_rows, across), BF16),
            vm((4, cache_rows, across), BF16),
            vm((rows, across), BF16),
            vm((rows, across), BF16),
            vm((2, rows, across), BF16),
            vm((rows, chans), BF16),
            vm((rows, chans), BF16),
            vm((rows, chans), F32),
            vm((groups, taps), F32),
            vm((groups // 2, rows, 2 * taps), BF16),
            vm((groups // 2, rows, 2 * taps), BF16),
            vm((rows, chans), F32),
            vm((heads, HD, rows), F32),
            vm((2 * heads, rows), F32),
            vm((2, heads, HD, rows), BF16),
            vm((2, heads, 2, rows), F32),
            vm((2, heads, HD, rows), BF16),
            vm((2, heads, 2, rows), F32),
            dma((12,)),
            dma((6,)),
            dma((6,)),
            dma((2, 2, heads)),
            dma((2, 2, heads)),
            dma((2, 3)),
            dma((2, 4)),
        ],
        compiler_params=pltpu.CompilerParams(
            collective_id=0, has_side_effects=True, vmem_limit_bytes=40 << 20
        ),
    )(
        *(
            pltpu.with_memory_space_constraint(array, pltpu.HBM)
            for array in (
                x_gate, x_key, x_value, conv_state, filter_taps,
                decay_rates.reshape(1, groups), skip_gain.reshape(1, chans),
                queries, stretch_keys, stretch_values, cache_keys, cache_values,
            )
        ),
        prefix_len,
    )
    return pl.pallas_call(
        store_kernel,
        out_shape=(
            jax.ShapeDtypeStruct((rows, chans), BF16),
            jax.ShapeDtypeStruct((rows, across), BF16),
        ),
        in_specs=[pl.BlockSpec(memory_space=pltpu.VMEM)] * 2,
        out_specs=(any_spec, any_spec),
        scratch_shapes=[dma((2,))],
        compiler_params=pltpu.CompilerParams(vmem_limit_bytes=40 << 20),
    )(*(pltpu.with_memory_space_constraint(array, pltpu.VMEM) for array in held))


def on_device(*arrays):
    rows, taps = arrays[0].shape[0], arrays[4].shape[1]
    if lax.axis_size("seq") == 4 and rows == taps == 128:
        return short_form(*arrays)
    return general_form(*arrays)


def solution(mesh):
    placed = (
        P(("parts", "seq"), "tp"),
        P(("parts", "seq"), "tp"),
        P(("parts", "seq"), "tp"),
        P("parts", "tp"),
        P("tp", None),
        P("tp"),
        P("tp"),
        P(("parts", "seq"), "tp"),
        P(("parts", "seq"), "tp"),
        P(("parts", "seq"), "tp"),
        P(("parts", "seq"), "tp"),
        P(("parts", "seq"), "tp"),
        P("parts"),
    )
    return jax.shard_map(
        on_device,
        mesh=mesh,
        in_specs=placed,
        out_specs=(P(("parts", "seq"), "tp"), P(("parts", "seq"), "tp")),
        check_vma=False,
    )
```

```python
import math

import jax
import jax.numpy as jnp
from jax import lax
from jax.experimental import pallas as pl
from jax.experimental.pallas import tpu as pltpu
from jax.sharding import PartitionSpec as P

HD = 128


far_position = 1 << 30


def shifted(value, axis, steps):
    count = lax.axis_size(axis)
    first, last = (max(0, -steps), min(count, count - steps))
    return lax.ppermute(value, axis, [(source, source + steps) for source in range(first, last)])


def general_form(
    x_gate,
    x_key,
    x_value,
    conv_state,
    filter_taps,
    decay_rates,
    skip_gain,
    queries,
    stretch_keys,
    stretch_values,
    cache_keys,
    cache_values,
    prefix_len,
):
    rows_dev = x_gate.shape[0]
    chans_dev = x_gate.shape[1]
    seq_index = lax.axis_index("seq")
    product_in = (x_key.astype(jnp.float32) * x_value.astype(jnp.float32)).astype(jnp.bfloat16)
    filter_reach = filter_taps.shape[1] - 1
    received = []
    taken = min(rows_dev, filter_reach)
    received.insert(0, shifted(product_in[rows_dev - taken :], "seq", 1))
    earlier = received[0]
    padded_state = jnp.concatenate(
        [conv_state, jnp.zeros((filter_reach, chans_dev), jnp.bfloat16)], axis=0
    )
    earlier = earlier + lax.dynamic_slice_in_dim(
        padded_state, seq_index * rows_dev, filter_reach, 0
    )
    extended = jnp.concatenate([earlier, product_in], axis=0)
    span_total = rows_dev + filter_reach
    tap_ramp = lax.iota(jnp.float32, filter_reach + 1)
    filters = (filter_taps * jnp.exp(-decay_rates[:, None] * tap_ramp[None, :])).astype(
        jnp.bfloat16
    )
    group_count = filters.shape[0]
    group_width = chans_dev // group_count
    skew_period = span_total + rows_dev - 1
    reversed_taps = jnp.concatenate(
        [filters[:, ::-1], jnp.zeros((group_count, skew_period - filter_reach - 1), jnp.bfloat16)],
        axis=1,
    )
    group_block = min(group_count, 16)
    conv_parts = []
    for first_group in range(0, group_count, group_block):
        taps_block = reversed_taps[first_group : first_group + group_block]
        toeplitz = jnp.tile(taps_block, (1, rows_dev + 1))[:, : rows_dev * (skew_period - 1)]
        toeplitz = toeplitz.reshape(group_block, rows_dev, skew_period - 1)[:, :, :span_total]
        columns = extended[:, first_group * group_width : (first_group + group_block) * group_width]
        columns = columns.reshape(span_total, group_block, group_width)
        conv_block = jnp.einsum(
            "gts,sgc->tgc", toeplitz, columns, preferred_element_type=jnp.float32
        )
        conv_parts.append(conv_block.reshape(rows_dev, group_block * group_width))
    filtered = jnp.concatenate(conv_parts, axis=1)
    hyena_out = (
        x_gate.astype(jnp.float32)
        * (filtered + skip_gain[None, :] * product_in.astype(jnp.float32))
    ).astype(jnp.bfloat16)
    head_count = queries.shape[1] // HD
    half_rows = rows_dev // 2
    scale_factor = 1.0 / math.sqrt(HD)
    half_ramp = lax.iota(jnp.int32, half_rows)
    second_base = seq_index * rows_dev + half_rows
    query_pos = jnp.stack([seq_index * rows_dev + half_ramp, second_base + half_ramp])
    query_heads = queries.reshape(2, half_rows, head_count, HD)
    limit_len = prefix_len[0]

    def consume(state, key_rows, value_rows, key_pos):
        row_total = key_rows.shape[0]
        if row_total <= 512:
            block_rows = row_total
            block_count = 1
        else:
            block_rows = 512
            block_count = -(-row_total // 512)
        key_blocks = key_rows.reshape(block_count, block_rows, head_count, HD)
        value_blocks = value_rows.reshape(block_count, block_rows, head_count, HD)
        pos_blocks = key_pos.reshape(block_count, block_rows)

        def one_block(block_step, inner):
            maxima, totals, sums = inner
            key_block = lax.dynamic_index_in_dim(key_blocks, block_step, 0, keepdims=False)
            value_block = lax.dynamic_index_in_dim(value_blocks, block_step, 0, keepdims=False)
            pos_block = lax.dynamic_index_in_dim(pos_blocks, block_step, 0, keepdims=False)
            for half_index in range(2):
                half_queries = query_heads[half_index]
                half_pos = query_pos[half_index]

                def update(parts):
                    run_max, run_total, run_sum = parts
                    scores = (
                        jnp.einsum(
                            "thd,shd->hts",
                            half_queries,
                            key_block,
                            preferred_element_type=jnp.float32,
                        )
                        * scale_factor
                    )
                    allowed = (pos_block[None, :] <= half_pos[:, None])[None]
                    scores = jnp.where(allowed, scores, -1e30)
                    new_max = jnp.maximum(run_max, jnp.max(scores, axis=2))
                    weights = jnp.where(allowed, jnp.exp(scores - new_max[:, :, None]), 0.0)
                    factor = jnp.exp(run_max - new_max)
                    new_total = run_total * factor + jnp.sum(weights, axis=2)
                    new_sum = run_sum * factor[:, :, None] + jnp.einsum(
                        "hts,shd->htd",
                        weights.astype(jnp.bfloat16),
                        value_block,
                        preferred_element_type=jnp.float32,
                    )
                    return (new_max, new_total, new_sum)

                def unchanged(parts):
                    return parts

                result = lax.cond(
                    jnp.min(pos_block) <= jnp.max(half_pos),
                    update,
                    unchanged,
                    (maxima[half_index], totals[half_index], sums[half_index]),
                )
                maxima = maxima.at[half_index].set(result[0])
                totals = totals.at[half_index].set(result[1])
                sums = sums.at[half_index].set(result[2])
            return (maxima, totals, sums)

        return lax.fori_loop(0, block_count, one_block, state)

    initial = (
        jnp.full((2, head_count, half_rows), -1e30, jnp.float32),
        jnp.zeros((2, head_count, half_rows), jnp.float32),
        jnp.zeros((2, head_count, half_rows, HD), jnp.float32),
    )
    cache_whole = (
        lax.all_gather(cache_keys, "seq", axis=0, tiled=True),
        lax.all_gather(cache_values, "seq", axis=0, tiled=True),
    )
    cache_ids = lax.iota(jnp.int32, cache_whole[0].shape[0])
    cache_pos = jnp.where(cache_ids < limit_len, -1, far_position)
    start_state = consume(initial, cache_whole[0], cache_whole[1], cache_pos)
    piece = (
        lax.all_gather(stretch_keys, "seq", axis=0, tiled=True),
        lax.all_gather(stretch_values, "seq", axis=0, tiled=True),
    )
    key_pos = lax.iota(jnp.int32, piece[0].shape[0])
    state = consume(start_state, piece[0], piece[1], key_pos)
    normalized = state[2] / state[1][:, :, :, None]
    result_rows = (
        normalized.transpose(0, 2, 1, 3).reshape(rows_dev, head_count * HD).astype(jnp.bfloat16)
    )
    return (hyena_out, result_rows)


MESH = pl.DeviceIdType.MESH
F32 = jnp.float32
BF16 = jnp.bfloat16


def remote(src, dst, send_sem, recv_sem, target):
    return pltpu.make_async_remote_copy(
        src_ref=src,
        dst_ref=dst,
        send_sem=send_sem,
        recv_sem=recv_sem,
        device_id={"seq": target},
        device_id_type=MESH,
    )


def short_kernel(
    x_gate, x_key, x_value, conv_state, filter_taps, decay_rates, skip_gain,
    queries, stretch_keys, stretch_values, cache_keys, cache_values, prefix_len,
    out_v, att_v,
    gate_v, key_v, value_v, state_v, taps_v, decay_v, skip_v, q_v, k_v, v_v,
    cache_k, cache_v, k_in, v_in, q_in, product_v, earlier_v, shifted_v,
    reversed_v, lower_v, upper_v, local_v,
    own_acc, own_stat, part_out, stat_out, part_in, stat_in,
    load_sem, send_sem, recv_sem, part_send, part_recv, cache_send, cache_recv, ready_sem,
):
    me = lax.axis_index("seq")
    rows, chans = gate_v.shape
    groups, taps = taps_v.shape
    width = chans // groups
    heads = q_v.shape[1] // HD
    scale_factor = 1.0 / math.sqrt(HD)

    loads = {}
    for at, (name, src, dst) in enumerate(
        [
            ("key", x_key, key_v),
            ("value", x_value, value_v),
            ("taps", filter_taps, taps_v),
            ("decay", decay_rates, decay_v),
            ("q", queries, q_v),
            ("k", stretch_keys, k_v),
            ("v", stretch_values, v_v),
            ("skip", skip_gain, skip_v),
            ("gate", x_gate, gate_v),
            ("state", conv_state, state_v),
            ("ck", cache_keys, cache_k.at[me]),
            ("cv", cache_values, cache_v.at[me]),
        ]
    ):
        loads[name] = pltpu.make_async_copy(src, dst, load_sem.at[at])
        loads[name].start()

    barrier = pltpu.get_barrier_semaphore()
    for step in range(1, 4):
        target = lax.rem(me + step, 4)

        @pl.when((target > 0) | (me == 1))
        def _():
            pl.semaphore_signal(
                barrier, inc=1, device_id={"seq": target}, device_id_type=MESH
            )

    @pl.when(me == 0)
    def _():
        pl.semaphore_wait(barrier, 1)

    @pl.when(me > 0)
    def _():
        pl.semaphore_wait(barrier, 3)

    @pl.when(me > 1)
    def _():
        pl.semaphore_signal(ready_sem, inc=1, device_id={"seq": 0}, device_id_type=MESH)

    send_k = remote(stretch_keys, k_in, send_sem.at[0], recv_sem.at[0], 1)
    send_v = remote(stretch_values, v_in, send_sem.at[1], recv_sem.at[1], 1)
    send_q2 = remote(queries, q_in.at[0], send_sem.at[2], recv_sem.at[2], 1)
    send_q3 = remote(queries, q_in.at[1], send_sem.at[3], recv_sem.at[3], 1)
    send_q3_near = remote(queries, q_in.at[1], send_sem.at[2], recv_sem.at[3], 2)
    send_product = [
        remote(
            product_v.at[:, pl.ds(half * chans // 2, chans // 2)],
            earlier_v.at[:, pl.ds(half * chans // 2, chans // 2)],
            send_sem.at[4 + half], recv_sem.at[4 + half], lax.rem(me + 1, 4),
        )
        for half in range(2)
    ]

    def send_part(slot, landing, head, target):
        return [
            remote(
                src.at[slot, head], dst.at[landing, head],
                part_send.at[which, slot, head], part_recv.at[which, landing, head], target,
            )
            for which, (src, dst) in enumerate([(part_out, part_in), (stat_out, stat_in)])
        ]

    @pl.when(me == 0)
    def _():
        send_k.start()
        send_v.start()

    @pl.when(me == 2)
    def _():
        send_q2.start()

    @pl.when(me == 3)
    def _():
        send_q3.start()
        send_q3_near.start()

    loads["key"].wait()
    loads["value"].wait()
    product_v[...] = (key_v[...].astype(F32) * value_v[...].astype(F32)).astype(BF16)

    @pl.when((me > 0) & (me < 3))
    def _():
        for copy in send_product:
            copy.start()

    @pl.when(me == 0)
    def _():
        pl.semaphore_wait(ready_sem, 2)

    cache_copies = []
    for step in range(1, 4):
        target = lax.rem(me + step, 4)
        for which, (src, dst) in enumerate(
            [(cache_keys, cache_k), (cache_values, cache_v)]
        ):
            copy = remote(
                src, dst.at[me], cache_send.at[which, step - 1], cache_recv.at[which, me], target
            )
            copy.start()
            cache_copies.append(copy)

    loads["taps"].wait()
    loads["decay"].wait()
    row_id = lax.broadcasted_iota(jnp.int32, (groups, groups), 0)
    col_id = lax.broadcasted_iota(jnp.int32, (groups, groups), 1)
    rates = jnp.sum(
        jnp.where(row_id == col_id, decay_v[...], 0.0), axis=1, keepdims=True
    )
    ramp = lax.broadcasted_iota(jnp.int32, (groups, taps), 1).astype(F32)
    filters = (taps_v[...] * jnp.exp(-rates * ramp)).astype(BF16)
    from_id = lax.broadcasted_iota(jnp.int32, (taps, taps), 0)
    to_id = lax.broadcasted_iota(jnp.int32, (taps, taps), 1)
    total_id = from_id + to_id
    flip = jnp.where((total_id == 0) | (total_id == taps), 1.0, 0.0).astype(BF16)
    reversed_v[...] = jnp.dot(filters, flip, preferred_element_type=F32)
    below = to_id <= from_id

    def build(pair, carry):
        for half in range(2):
            row = reversed_v[pl.ds(pair * 2 + half, 1), :]
            circ = pltpu.roll(
                jnp.broadcast_to(row, (rows, taps)), 0, 1, stride=1, stride_axis=0
            )
            lanes = pl.ds(half * taps, taps)
            lower_v[pair, :, lanes] = jnp.where(below, circ, 0.0).astype(BF16)
            upper_v[pair, :, lanes] = jnp.where(below, 0.0, circ).astype(BF16)
        return carry

    lax.fori_loop(0, groups // 2, build, 0)

    lane = lax.broadcasted_iota(jnp.int32, (1, 128), 1)
    odd_lane = lax.rem(lane // width, 2) == 1
    odd = jnp.where(odd_lane, 1.0, 0.0).astype(BF16)
    even = jnp.where(odd_lane, 0.0, 1.0).astype(BF16)
    pair_of = lax.broadcasted_iota(jnp.int32, (rows, 128), 1) // (2 * width)
    pairs = 128 // (2 * width)

    def filtered(matrix_ref, block, tile):
        stacked = jnp.concatenate([block * even, block * odd], axis=0)
        total = None
        for at in range(pairs):
            term = jnp.dot(
                matrix_ref[tile * pairs + at], stacked, preferred_element_type=F32
            )
            total = term if total is None else jnp.where(pair_of == at, term, total)
        return total

    loads["skip"].wait()
    for tile in range(chans // 128):
        cols = slice(tile * 128, (tile + 1) * 128)
        block = product_v[:, cols]
        local_v[:, cols] = filtered(lower_v, block, tile) + skip_v[:, cols] * block.astype(F32)

    @pl.when(me == 0)
    def _():
        send_k.wait_send()
        send_v.wait_send()
        for copy in send_product:
            copy.start()

    loads["q"].wait()
    loads["k"].wait()
    loads["v"].wait()
    loads["ck"].wait()
    loads["cv"].wait()
    for step in range(1, 4):
        source = lax.rem(me + step, 4)
        for which, (src, dst) in enumerate(
            [(cache_keys, cache_k), (cache_values, cache_v)]
        ):
            remote(
                src, dst.at[source], cache_send.at[which, step - 1],
                cache_recv.at[which, source], source,
            ).wait_recv()

    def joined(ref, cols):
        return jnp.concatenate(
            [ref[at, :, cols].astype(F32) for at in range(4)], axis=0
        ).astype(BF16)

    cache_rows = 4 * cache_k.shape[1]
    causal = to_id >= from_id
    in_prefix = (
        lax.broadcasted_iota(jnp.int32, (cache_rows, rows), 0) < prefix_len[0]
    )

    def attend(query, blocks):
        scores = []
        for key, value, allowed in blocks:
            score = (
                lax.dot_general(
                    key, query, (((1,), (1,)), ((), ())), preferred_element_type=F32
                )
                * scale_factor
            )
            if allowed is not None:
                score = jnp.where(allowed, score, -1e30)
            scores.append(score)
        top = jnp.max(scores[0], axis=0, keepdims=True)
        for score in scores[1:]:
            top = jnp.maximum(top, jnp.max(score, axis=0, keepdims=True))
        total, mixed = 0.0, 0.0
        for score, (key, value, allowed) in zip(scores, blocks):
            weight = jnp.exp(score - top)
            if allowed is not None:
                weight = jnp.where(allowed, weight, 0.0)
            total = total + jnp.sum(weight, axis=0, keepdims=True)
            mixed = mixed + lax.dot_general(
                value, weight.astype(BF16), (((0,), (0,)), ((), ())),
                preferred_element_type=F32,
            )
        return top, total, mixed

    def head_cols(head):
        return slice(head * HD, (head + 1) * HD)

    def own_blocks(head):
        cols = head_cols(head)
        return [
            (joined(cache_k, cols), joined(cache_v, cols), in_prefix),
            (k_v[:, cols], v_v[:, cols], causal),
        ]

    def keep(head, result):
        own_stat[head : head + 1, :] = result[0]
        own_stat[heads + head : heads + head + 1, :] = result[1]
        own_acc[head] = result[2]

    def give(slot, head, result):
        stat_out[slot, head, 0:1, :] = result[0]
        stat_out[slot, head, 1:2, :] = result[1]
        part_out[slot, head] = (result[2] / result[1]).astype(BF16)

    @pl.when(me != 1)
    def _():
        for head in range(heads):
            keep(head, attend(q_v[:, head_cols(head)], own_blocks(head)))

    @pl.when(me == 1)
    def _():
        send_k.wait_recv()
        send_v.wait_recv()

        def shared_blocks(cols):
            return [
                (k_in[:, cols], v_in[:, cols], None),
                (k_v[:, cols], v_v[:, cols], None),
            ]

        for slot, arrival, target in ((0, send_q2, 2), (1, send_q3, 3)):
            arrival.wait_recv()
            for head in range(heads):
                cols = head_cols(head)
                give(slot, head, attend(q_in[slot, :, cols], shared_blocks(cols)))
                for copy in send_part(slot, 0, head, target):
                    copy.start()
        for head in range(heads):
            cols = head_cols(head)
            keep(
                head,
                attend(
                    q_v[:, cols], own_blocks(head) + [(k_in[:, cols], v_in[:, cols], None)]
                ),
            )

    @pl.when(me == 2)
    def _():
        send_q3_near.wait_recv()
        for head in range(heads):
            cols = head_cols(head)
            give(1, head, attend(q_in[1, :, cols], [(k_v[:, cols], v_v[:, cols], None)]))
            for copy in send_part(1, 1, head, 3):
                copy.start()

    loads["state"].wait()

    @pl.when(me == 0)
    def _():
        shifted_v[0:1, :] = jnp.zeros((1, chans), F32)
        shifted_v[pl.ds(1, rows - 1), :] = state_v[...].astype(F32)
        earlier_v[...] = shifted_v[...].astype(BF16)

    loads["gate"].wait()
    tiles = chans // 128
    for tile in range(tiles):
        if tile % (tiles // 2) == 0:

            @pl.when(me > 0)
            def _():
                send_product[tile // (tiles // 2)].wait_recv()

        cols = slice(tile * 128, (tile + 1) * 128)
        whole = local_v[:, cols] + filtered(upper_v, earlier_v[:, cols], tile)
        out_v[:, cols] = (gate_v[:, cols].astype(F32) * whole).astype(BF16)

    def finish(slots):
        for head in range(heads):
            for slot in slots:
                for copy in send_part(1, slot, head, 1):
                    copy.wait_recv()
            top = own_stat[head : head + 1, :]
            tops = [stat_in[slot, head, 0:1, :] for slot in slots]
            best = top
            for other in tops:
                best = jnp.maximum(best, other)
            share = jnp.exp(top - best)
            total = own_stat[heads + head : heads + head + 1, :] * share
            mixed = own_acc[head] * share
            for slot, other in zip(slots, tops):
                share = stat_in[slot, head, 1:2, :] * jnp.exp(other - best)
                total = total + share
                mixed = mixed + part_in[slot, head].astype(F32) * share
            att_v[:, head_cols(head)] = (mixed / total).T.astype(BF16)

    @pl.when(me < 2)
    def _():
        finish([])

    @pl.when(me == 2)
    def _():
        finish([0])

    @pl.when(me == 3)
    def _():
        finish([1, 0])

    for copy in cache_copies:
        copy.wait_send()

    @pl.when(me < 3)
    def _():
        for copy in send_product:
            copy.wait_send()

    @pl.when(me == 1)
    def _():
        for head in range(heads):
            for copy in send_part(1, 0, head, 3) + send_part(0, 0, head, 2):
                copy.wait_send()

    @pl.when(me == 2)
    def _():
        send_q2.wait_send()
        for head in range(heads):
            for copy in send_part(1, 1, head, 3):
                copy.wait_send()

    @pl.when(me == 3)
    def _():
        send_q3.wait_send()
        send_q3_near.wait_send()


def store_kernel(hyena_in, attention_in, hyena_out, attention_out, sem):
    copies = [
        pltpu.make_async_copy(hyena_in, hyena_out, sem.at[0]),
        pltpu.make_async_copy(attention_in, attention_out, sem.at[1]),
    ]
    for copy in copies:
        copy.start()
    for copy in copies:
        copy.wait()


def short_form(
    x_gate, x_key, x_value, conv_state, filter_taps, decay_rates, skip_gain,
    queries, stretch_keys, stretch_values, cache_keys, cache_values, prefix_len,
):
    rows, chans = x_gate.shape
    groups, taps = filter_taps.shape
    across = queries.shape[1]
    heads = across // HD
    cache_rows = cache_keys.shape[0]
    any_spec = pl.BlockSpec(memory_space=pltpu.HBM)
    dma = pltpu.SemaphoreType.DMA
    vm = pltpu.VMEM
    held = pl.pallas_call(
        short_kernel,
        out_shape=(
            pltpu.VMEM((rows, chans), BF16),
            pltpu.VMEM((rows, across), BF16),
        ),
        in_specs=[any_spec] * 12 + [pl.BlockSpec(memory_space=pltpu.SMEM)],
        out_specs=(pl.BlockSpec(memory_space=pltpu.VMEM),) * 2,
        scratch_shapes=[
            vm((rows, chans), BF16),
            vm((rows, chans), BF16),
            vm((rows, chans), BF16),
            vm((rows - 1, chans), BF16),
            vm((groups, taps), F32),
            vm((1, groups), F32),
            vm((1, chans), F32),
            vm((rows, across), BF16),
            vm((rows, across), BF16),
            vm((rows, across), BF16),
            vm((4, cache_rows, across), BF16),
            vm((4, cache_rows, across), BF16),
            vm((rows, across), BF16),
            vm((rows, across), BF16),
            vm((2, rows, across), BF16),
            vm((rows, chans), BF16),
            vm((rows, chans), BF16),
            vm((rows, chans), F32),
            vm((groups, taps), F32),
            vm((groups // 2, rows, 2 * taps), BF16),
            vm((groups // 2, rows, 2 * taps), BF16),
            vm((rows, chans), F32),
            vm((heads, HD, rows), F32),
            vm((2 * heads, rows), F32),
            vm((2, heads, HD, rows), BF16),
            vm((2, heads, 2, rows), F32),
            vm((2, heads, HD, rows), BF16),
            vm((2, heads, 2, rows), F32),
            dma((12,)),
            dma((6,)),
            dma((6,)),
            dma((2, 2, heads)),
            dma((2, 2, heads)),
            dma((2, 3)),
            dma((2, 4)),
            pltpu.SemaphoreType.REGULAR,
        ],
        compiler_params=pltpu.CompilerParams(
            collective_id=0, has_side_effects=True, vmem_limit_bytes=40 << 20
        ),
    )(
        *(
            pltpu.with_memory_space_constraint(array, pltpu.HBM)
            for array in (
                x_gate, x_key, x_value, conv_state, filter_taps,
                decay_rates.reshape(1, groups), skip_gain.reshape(1, chans),
                queries, stretch_keys, stretch_values, cache_keys, cache_values,
            )
        ),
        prefix_len,
    )
    return pl.pallas_call(
        store_kernel,
        out_shape=(
            jax.ShapeDtypeStruct((rows, chans), BF16),
            jax.ShapeDtypeStruct((rows, across), BF16),
        ),
        in_specs=[pl.BlockSpec(memory_space=pltpu.VMEM)] * 2,
        out_specs=(any_spec, any_spec),
        scratch_shapes=[dma((2,))],
        compiler_params=pltpu.CompilerParams(vmem_limit_bytes=40 << 20),
    )(*(pltpu.with_memory_space_constraint(array, pltpu.VMEM) for array in held))


def on_device(*arrays):
    rows, taps = arrays[0].shape[0], arrays[4].shape[1]
    if lax.axis_size("seq") == 4 and rows == taps == 128:
        return short_form(*arrays)
    return general_form(*arrays)


def solution(mesh):
    placed = (
        P(("parts", "seq"), "tp"),
        P(("parts", "seq"), "tp"),
        P(("parts", "seq"), "tp"),
        P("parts", "tp"),
        P("tp", None),
        P("tp"),
        P("tp"),
        P(("parts", "seq"), "tp"),
        P(("parts", "seq"), "tp"),
        P(("parts", "seq"), "tp"),
        P(("parts", "seq"), "tp"),
        P(("parts", "seq"), "tp"),
        P("parts"),
    )
    return jax.shard_map(
        on_device,
        mesh=mesh,
        in_specs=placed,
        out_specs=(P(("parts", "seq"), "tp"), P(("parts", "seq"), "tp")),
        check_vma=False,
    )
```
